256 devices in a mesh: fsdp: 32 (over y, x, core), tp: 8 (over z).
Axes of the slice: x: 4, y: 4, z: 8, core: 2. Of those that a mesh axis runs over, the one named last changes fastest.
Arguments:
- learner_flat: bfloat16 [2, 159383552], P(None, ('fsdp', 'tp')), may hold values from -1.796875 to 1.796875
- param_offsets: int32 [2, 128, 4], replicated, may hold values from 0 to 622336, as said below
- owner_map: int32 [2, 128], replicated, may hold values from 0 to 31, as said below
- slice_map: int32 [32, 8], replicated, may hold values from 0 to 7, each once within a row
Outputs:
- query_absorbed: bfloat16 [2, 128, 1536, 512], P(None, 'fsdp', 'tp')
- output_absorbed: bfloat16 [2, 128, 7168, 512], P(None, 'fsdp', 'tp')
The draws below stay inside these ranges and needn't reach their ends.
Inputs may be any that keep to these rules, and one draw needn't show every extreme that they name: `param_offsets`: in each layer the pieces of all heads' four parameters lie in a rank's 622592 entries one after another in some order, without gaps or intersections; a piece of a parameter holds that parameter's entries divided by 256; the last piece of each layer is a key up-projection piece. `owner_map`: in each layer every index of fsdp owns exactly 4 heads.
All inputs are finite; a program needn't handle non-finite values.
Results may differ from the reference program's by a relative error of at most 0.001.
Values may be sent and summed in bfloat16 or wider, within the bound.
A program may use at most 64 MiB of HBM per device.

```python
import jax
import jax.numpy as jnp
from jax import lax

D = 7168
QR = 1536
KVR = 512
QK_NOPE = 128
V_DIM = 128
HEAD_DEV = 4
LAYERS = 2
HEADS = 128
RANKS = 256
REC = 1245184
SHARD = 622592
Q_SLICE = 192
O_SLICE = 896
N_FSDP = 32
N_TP = 8


def draw_param_offsets(key, part):
    piece_sizes = jnp.array([QR * QK_NOPE // RANKS, QK_NOPE * KVR // RANKS, V_DIM * KVR // RANKS, D * V_DIM // RANKS], dtype=jnp.int32)
    layer_keys = jax.random.split(jax.random.fold_in(key, 11), LAYERS)
    piece_count = HEADS * 4

    def one_layer(layer_key):
        order_key, pick_key = jax.random.split(layer_key)
        piece_order = jax.random.permutation(order_key, piece_count).astype(jnp.int32)
        target = (jax.random.randint(pick_key, (), 0, HEADS) * 4 + 1).astype(jnp.int32)
        position = jnp.argmax((piece_order == target).astype(jnp.int32)).astype(jnp.int32)
        last_value = piece_order[piece_count - 1]
        piece_order = piece_order.at[position].set(last_value).at[piece_count - 1].set(target)
        sizes_here = jnp.tile(piece_sizes, HEADS)[piece_order]
        start_at = (jnp.cumsum(sizes_here) - sizes_here).astype(jnp.int32)
        placed = jnp.zeros((piece_count,), dtype=jnp.int32).at[piece_order].set(start_at)
        return placed.reshape(HEADS, 4)
    return jax.vmap(one_layer)(layer_keys)


def draw_owner_map(key, part):
    layer_keys = jax.random.split(jax.random.fold_in(key, 23), LAYERS)

    def one_layer(layer_key):
        return (jax.random.permutation(layer_key, HEADS) // HEAD_DEV).astype(jnp.int32)
    return jax.vmap(one_layer)(layer_keys)


def block_scale(key, dims, cuts, smallest, largest):
    def one(axis_at, blocks):
        heights = jax.random.uniform(jax.random.fold_in(jax.random.fold_in(key, 6), axis_at), (blocks,), jnp.float32, smallest / len(cuts), largest / len(cuts))
        return jnp.repeat(jnp.exp(heights), dims[axis_at] // blocks).reshape((-1,) + (1,) * (len(dims) - axis_at - 1))

    gain = one(*cuts[0])
    for cut in cuts[1:]:
        gain = gain * one(*cut)
    return gain


def normal_values(stream_key, shape, deviation, reach, cuts=(), kind=jnp.bfloat16):
    values = deviation * jax.random.normal(stream_key, shape, jnp.float32)
    if cuts:
        values = values * block_scale(stream_key, shape, cuts, -0.22, 0.18)
    return jnp.clip(values, -reach, reach).astype(kind)


def setup_inputs(seed: int = 0) -> dict:
    key_list = jax.random.split(jax.random.key(seed), 5)
    return {
        "learner_flat": normal_values(key_list[0], (LAYERS, HEADS * REC), 0.3, 1.796875, ((1, 256),)),
        "param_offsets": draw_param_offsets(jax.random.fold_in(key_list[4], 71), 0),
        "owner_map": draw_owner_map(jax.random.fold_in(key_list[4], 71), 0),
        "slice_map": jax.vmap(lambda own: jax.random.permutation(own, N_TP))(jax.random.split(key_list[3], N_FSDP)).reshape((N_FSDP, N_TP)).astype(jnp.int32),
    }


def head_order(owner_map, per_group):
    head_count = owner_map.shape[1]
    head_index = jnp.arange(head_count, dtype=jnp.int32)
    same_owner = owner_map[:, :, None] == owner_map[:, None, :]
    before = head_index[None, None, :] < head_index[None, :, None]
    head_rank = jnp.sum(jnp.logical_and(same_owner, before).astype(jnp.int32), axis=2)
    head_slot = owner_map * per_group + head_rank
    slot_hits = head_slot[:, :, None] == head_index[None, None, :]
    return jnp.sum(jnp.where(slot_hits, head_index[None, :, None], 0), axis=1).astype(jnp.int32)


def reference(learner_flat, param_offsets, owner_map, slice_map):
    widths = (QR * QK_NOPE // RANKS, QK_NOPE * KVR // RANKS, V_DIM * KVR // RANKS, D * V_DIM // RANKS)
    head_at = head_order(owner_map, HEAD_DEV)
    query_layers = []
    output_layers = []
    for layer_id in range(LAYERS):
        flat_table = learner_flat[layer_id].reshape(RANKS, SHARD)

        def one_head(slot_id):
            head_id = head_at[layer_id, slot_id]
            begins = param_offsets[layer_id, head_id]

            def fetch_param(kind_id, param_shape):
                pieces = lax.dynamic_slice(flat_table, (jnp.int32(0), begins[kind_id].astype(jnp.int32)), (RANKS, widths[kind_id]))
                return pieces.reshape(param_shape).astype(jnp.float32)

            query_up = fetch_param(0, (QR, QK_NOPE))
            key_up = fetch_param(1, (QK_NOPE, KVR))
            value_up = fetch_param(2, (V_DIM, KVR))
            out_proj = fetch_param(3, (D, V_DIM))
            absorbed_query = jnp.dot(query_up, key_up, precision=lax.Precision.HIGHEST, preferred_element_type=jnp.float32)
            absorbed_output = jnp.dot(out_proj, value_up, precision=lax.Precision.HIGHEST, preferred_element_type=jnp.float32)
            row_order = slice_map[slot_id // HEAD_DEV]
            absorbed_query = jnp.take(absorbed_query.reshape(N_TP, Q_SLICE, KVR), row_order, axis=0).reshape(QR, KVR)
            absorbed_output = jnp.take(absorbed_output.reshape(N_TP, O_SLICE, KVR), row_order, axis=0).reshape(D, KVR)
            return absorbed_query.astype(jnp.bfloat16), absorbed_output.astype(jnp.bfloat16)

        query_here, output_here = lax.map(one_head, jnp.arange(HEADS, dtype=jnp.int32))
        query_layers.append(query_here)
        output_layers.append(output_here)
    return jnp.stack(query_layers, axis=0), jnp.stack(output_layers, axis=0)
```

```python
import functools

import jax
import jax.numpy as jnp
from jax import lax
from jax.experimental import pallas as pl
from jax.experimental.pallas import tpu as pltpu
from jax.sharding import PartitionSpec as P

MESH = pl.DeviceIdType.MESH

LANES = 128
D = 7168
QR = 1536
KVR = 512
QK_NOPE = 128
V_DIM = 128
LAYERS = 2
HEADS = 128
FSDP = 32
TP = 8
PER_GROUP = HEADS // FSDP
RANKS = FSDP * TP
Q_ROWS = QR * QK_NOPE // RANKS // LANES
KV_ROWS = QK_NOPE * KVR // RANKS // LANES
O_ROWS = D * V_DIM // RANKS // LANES
SHARD_ROWS = HEADS * (Q_ROWS + 2 * KV_ROWS + O_ROWS)
CHUNKS = LAYERS * PER_GROUP
QUARTER = FSDP // TP
PAD = 16


def gather_kernel(owner, offs, x_ref, chunk_ref, small_ref, flat, small, count):
    step_rows = 512

    def widen(i, carry):
        at = pl.multiple_of(i * step_rows, step_rows)
        flat[pl.ds(PAD + at, step_rows), :] = x_ref[pl.ds(at, step_rows), :].astype(jnp.float32)
        return carry

    lax.fori_loop(0, LAYERS * SHARD_ROWS // step_rows, widen, 0)

    def clear(i, carry):
        count[i] = 0
        return carry

    lax.fori_loop(0, LAYERS * FSDP, clear, 0)
    low = lax.broadcasted_iota(jnp.int32, (8, LANES), 0) < 4

    for l in range(LAYERS):

        def one_head(h, carry, l=l):
            f = owner[l, h]
            j = count[l * FSDP + f]
            count[l * FSDP + f] = j + 1
            starts = [PAD + l + 2 * (offs[l, k, h] // LANES) for k in range(4)]

            def rows(k, first, n):
                return flat[pl.ds(starts[k] + 2 * first, n, stride=2), :]

            for i in range(3):
                chunk_ref[l, j, f, i] = rows(3, 8 * i, 8).astype(jnp.bfloat16)
            mixed = jnp.where(low, rows(3, 24, 8), rows(0, -4, 8))
            chunk_ref[l, j, f, 3] = mixed.astype(jnp.bfloat16)
            base = (l * FSDP + f) * 24
            small[pl.ds(base + 2 * j, 2), :] = rows(0, 4, 2)
            small[pl.ds(base + 8 + 4 * j, 2), :] = rows(1, 0, 2)
            small[pl.ds(base + 10 + 4 * j, 2), :] = rows(2, 0, 2)
            return carry

        lax.fori_loop(0, HEADS, one_head, 0, unroll=4)

    for l in range(LAYERS):

        def narrow(f, carry, l=l):
            at = pl.multiple_of((l * FSDP + f) * 24, 8)
            small_ref[l, f] = small[pl.ds(at, 24), :].astype(jnp.bfloat16).reshape(3, 8, LANES)
            return carry

        lax.fori_loop(0, FSDP, narrow, 0)


def gather(owner_map, param_offsets, learner_flat):
    x = learner_flat.reshape(LAYERS, SHARD_ROWS, LANES).transpose(1, 0, 2).reshape(LAYERS * SHARD_ROWS, LANES)
    vmem = pl.BlockSpec(memory_space=pltpu.VMEM)
    smem = pl.BlockSpec(memory_space=pltpu.SMEM)
    return pl.pallas_call(
        gather_kernel,
        out_shape=(
            jax.ShapeDtypeStruct((LAYERS, PER_GROUP, FSDP, 4, 8, LANES), jnp.bfloat16),
            jax.ShapeDtypeStruct((LAYERS, FSDP, 3, 8, LANES), jnp.bfloat16),
        ),
        in_specs=[smem, smem, vmem],
        out_specs=(vmem, vmem),
        scratch_shapes=[
            pltpu.VMEM((LAYERS * SHARD_ROWS + 2 * PAD, LANES), jnp.float32),
            pltpu.VMEM((LAYERS * FSDP * 24, LANES), jnp.float32),
            pltpu.SMEM((LAYERS * FSDP,), jnp.int32),
        ],
        compiler_params=pltpu.CompilerParams(vmem_limit_bytes=40 << 20),
    )(owner_map, param_offsets.transpose(0, 2, 1), x)


def exchange_kernel(slices, chunk_ref, small_ref, q_ref, o_ref, k_ref, v_ref, *scratch):
    scratch = list(scratch)

    def take(n):
        out = scratch[:n]
        del scratch[:n]
        return out

    land_chunk = take(CHUNKS)
    land_small = take(LAYERS)
    send_rows = take(CHUNKS)
    send_rest = take(LAYERS)
    got_rows = take(CHUNKS)
    got_rest = take(LAYERS)
    got_kv = take(LAYERS)
    o_wide, q_wide, kv_wide, kv_out = take(4)
    sems = take(len(scratch))
    (
        chunk_sent, chunk_here, small_sent, small_here, rows_sent, rows_here, rest_sent, rest_here, ring_sent, ring_here, own_here,
    ) = sems

    f = lax.axis_index("fsdp")
    t = lax.axis_index("tp")

    barrier = pltpu.get_barrier_semaphore()

    def greet_plane(d, carry):
        pl.semaphore_signal(barrier, inc=1, device_id=(lax.rem(f + d, FSDP), t), device_id_type=MESH)
        return carry

    def greet_line(d, carry):
        pl.semaphore_signal(barrier, inc=1, device_id=(f, lax.rem(t + d, TP)), device_id_type=MESH)
        return carry

    lax.fori_loop(1, FSDP, greet_plane, 0)
    lax.fori_loop(1, TP, greet_line, 0)
    pl.semaphore_wait(barrier, FSDP - 1 + TP - 1)

    def remote(src, dst, send_sem, recv_sem, device):
        return pltpu.make_async_remote_copy(
            src_ref=src, dst_ref=dst, send_sem=send_sem, recv_sem=recv_sem, device_id=device, device_id_type=MESH
        )

    def spread_plane(src, dst, send_sem, recv_sem):
        pltpu.make_async_copy(src.at[f], dst.at[f], recv_sem).start()

        def one(d, carry):
            to = lax.rem(f + d, FSDP)
            remote(src.at[to], dst.at[f], send_sem, recv_sem, (to, t)).start()
            return carry

        lax.fori_loop(1, FSDP, one, 0)

    def spread_line(src, dst, send_sem, recv_sem):
        pltpu.make_async_copy(src.at[t], dst.at[t], recv_sem).start()

        def one(d, carry):
            to = lax.rem(t + d, TP)
            remote(src.at[to], dst.at[t], send_sem, recv_sem, (f, to)).start()
            return carry

        lax.fori_loop(1, TP, one, 0)

    def all_arrived(dst, recv_sem):
        pltpu.make_async_copy(dst, dst, recv_sem).wait()

    def all_left(src, n, send_sem):
        pltpu.make_async_copy(src.at[pl.ds(0, n)], src.at[pl.ds(0, n)], send_sem).wait()

    def send_small(l):
        spread_plane(small_ref.at[l], land_small[l], small_sent.at[l], small_here.at[l])

    def send_chunk(c):
        spread_plane(chunk_ref.at[c // PER_GROUP, c % PER_GROUP], land_chunk[c], chunk_sent.at[c], chunk_here.at[c])

    def forward_rows(c):
        all_arrived(land_chunk[c], chunk_here.at[c])

        def one(to, carry):
            first = slices[f, to] * QUARTER
            for q in range(QUARTER):
                send_rows[c][to, pl.ds(4 * q, 4)] = land_chunk[c][first + q]
            return carry

        lax.fori_loop(0, TP, one, 0)
        spread_line(send_rows[c], got_rows[c], rows_sent.at[c], rows_here.at[c])

    def forward_rest(l):
        def one(to, carry):
            first = slices[f, to] * QUARTER
            for q in range(QUARTER):
                send_rest[l][to, q] = land_small[l][first + q, 0]
            return carry

        lax.fori_loop(0, TP, one, 0)
        spread_line(send_rest[l], got_rest[l], rest_sent.at[l], rest_here.at[l])

    half = FSDP // 2
    steps = TP // 2
    up = lax.rem(t + 1, TP)
    down = lax.rem(t + TP - 1, TP)

    def ring_copy(l, direction, step):
        origin = lax.rem(t + (TP - step if direction == 0 else step), TP)
        if step == steps - 1:
            part = pl.ds(0, half) if direction == 0 else pl.ds(half, half)
        else:
            part = pl.ds(0, FSDP)
        to = got_kv[l].at[origin, part]
        src = land_small[l].at[part, pl.ds(1, 2)] if step == 0 else to
        return remote(src, to, ring_sent.at[l, direction, step], ring_here.at[l, direction, step], (f, up if direction == 0 else down))

    def ring_start(l, step):
        if step == 0:
            pltpu.make_async_copy(land_small[l].at[:, pl.ds(1, 2)], got_kv[l].at[t], own_here.at[l]).start()
        for direction in range(2):
            if step:
                ring_copy(l, direction, step - 1).wait_recv()
            ring_copy(l, direction, step).start()

    def ring_end(l):
        for direction in range(2):
            ring_copy(l, direction, steps - 1).wait_recv()
        pltpu.make_async_copy(land_small[l].at[:, pl.ds(1, 2)], got_kv[l].at[t], own_here.at[l]).wait()

    def assemble_kv(l):
        def widen(i, carry):
            ti = i // FSDP
            fi = i % FSDP
            rows = pl.ds(pl.multiple_of(i * 16, 16), 16)
            kv_wide[rows, :] = got_kv[l][ti, fi].astype(jnp.float32).reshape(16, LANES)
            return carry

        lax.fori_loop(0, TP * FSDP, widen, 0)

        def one_head(j, carry):
            for which, out_ref in ((0, k_ref), (1, v_ref)):
                for b in range(4):
                    for u in range(4):
                        first = (2 * u + b // 2) * FSDP * 16 + 4 * j + 2 * which + b % 2
                        kv_out[pl.ds(u, FSDP, stride=4), :] = kv_wide[pl.ds(first, FSDP, stride=16), :]
                    out_ref[l, j, :, pl.ds(b * LANES, LANES)] = kv_out[...].astype(jnp.bfloat16)
            return carry

        lax.fori_loop(0, PER_GROUP, one_head, 0)

    def assemble_rows(c):
        l, j = c // PER_GROUP, c % PER_GROUP
        all_arrived(got_rows[c], rows_here.at[c])
        if j == 0:
            all_arrived(got_rest[l], rest_here.at[l])

        def one(ti, carry):
            for q in range(QUARTER):
                block = got_rows[c][ti, pl.ds(4 * q, 4)].astype(jnp.float32).reshape(32, LANES)
                o_wide[pl.ds(q * TP * O_ROWS + ti * O_ROWS, O_ROWS), :] = block[:O_ROWS]
                q_wide[pl.ds(q * TP * Q_ROWS + ti * Q_ROWS, 4), :] = block[O_ROWS:]
                rest = got_rest[l][ti, q].astype(jnp.float32)
                q_wide[pl.ds(q * TP * Q_ROWS + ti * Q_ROWS + 4, 2), :] = rest[2 * j : 2 * j + 2]
            return carry

        lax.fori_loop(0, TP, one, 0)
        o_ref[l, j] = o_wide[...].astype(jnp.bfloat16)
        q_ref[l, j] = q_wide[...].astype(jnp.bfloat16)

    ahead = 2
    send_small(0)
    send_chunk(0)
    send_small(1)
    for c in range(1, ahead):
        send_chunk(c)
    for c in range(CHUNKS):
        if c + ahead < CHUNKS:
            send_chunk(c + ahead)
        if c == 0:
            all_arrived(land_small[0], small_here.at[0])
            forward_rest(0)
            ring_start(0, 0)
        forward_rows(c)
        if c == 0:
            all_arrived(land_small[1], small_here.at[1])
            forward_rest(1)
            ring_start(1, 0)
        elif c < steps:
            ring_start(0, c)
            ring_start(1, c)
        if c == steps:
            ring_end(0)
            assemble_kv(0)
        if c == steps + 1:
            ring_end(1)
            assemble_kv(1)
        if c >= 1:
            assemble_rows(c - 1)
    assemble_rows(CHUNKS - 1)

    for c in range(CHUNKS):
        all_left(land_chunk[c], FSDP - 1, chunk_sent.at[c])
        all_left(send_rows[c], TP - 1, rows_sent.at[c])
    for l in range(LAYERS):
        all_left(land_small[l], FSDP - 1, small_sent.at[l])
        all_left(send_rest[l], TP - 1, rest_sent.at[l])
        for direction in range(2):
            for step in range(steps):
                ring_copy(l, direction, step).wait_send()


def exchange(slice_map, chunks, small):
    vmem = pl.BlockSpec(memory_space=pltpu.VMEM)
    bf16 = jnp.bfloat16
    dma = pltpu.SemaphoreType.DMA
    rows_o = D // TP
    rows_q = QR // TP
    ring = (LAYERS, 2, TP // 2)
    return pl.pallas_call(
        exchange_kernel,
        out_shape=(
            jax.ShapeDtypeStruct((LAYERS, PER_GROUP, rows_q, LANES), bf16),
            jax.ShapeDtypeStruct((LAYERS, PER_GROUP, rows_o, LANES), bf16),
            jax.ShapeDtypeStruct((LAYERS, PER_GROUP, QK_NOPE, KVR), bf16),
            jax.ShapeDtypeStruct((LAYERS, PER_GROUP, V_DIM, KVR), bf16),
        ),
        in_specs=[pl.BlockSpec(memory_space=pltpu.SMEM), vmem, vmem],
        out_specs=(vmem,) * 4,
        scratch_shapes=[pltpu.VMEM((FSDP, 4, 8, LANES), bf16)] * CHUNKS
        + [pltpu.VMEM((FSDP, 3, 8, LANES), bf16)] * LAYERS
        + [pltpu.VMEM((TP, 16, 8, LANES), bf16)] * CHUNKS
        + [pltpu.VMEM((TP, 4, 8, LANES), bf16)] * LAYERS
        + [pltpu.VMEM((TP, 16, 8, LANES), bf16)] * CHUNKS
        + [pltpu.VMEM((TP, 4, 8, LANES), bf16)] * LAYERS
        + [pltpu.VMEM((TP, FSDP, 2, 8, LANES), bf16)] * LAYERS
        + [
            pltpu.VMEM((rows_o, LANES), jnp.float32),
            pltpu.VMEM((rows_q, LANES), jnp.float32),
            pltpu.VMEM((TP * FSDP * 16, LANES), jnp.float32),
            pltpu.VMEM((QK_NOPE, LANES), jnp.float32),
            dma((CHUNKS,)), dma((CHUNKS,)), dma((LAYERS,)), dma((LAYERS,)),
            dma((CHUNKS,)), dma((CHUNKS,)), dma((LAYERS,)), dma((LAYERS,)),
            dma(ring), dma(ring), dma((LAYERS,)),
        ],
        compiler_params=pltpu.CompilerParams(collective_id=0, has_side_effects=True, vmem_limit_bytes=50 << 20),
    )(slice_map, chunks, small)


def per_device(learner_flat, param_offsets, owner_map, slice_map):
    chunks, small = gather(owner_map, param_offsets, learner_flat)
    query, out, key, value = exchange(slice_map, chunks, small)

    def product(a, b):
        return jnp.einsum("lhrc,lhck->lhrk", a, b, preferred_element_type=jnp.float32).astype(jnp.bfloat16)

    return product(query, key), product(out, value)


def solution(mesh):
    placed = (P(None, ("fsdp", "tp")), P(), P(), P())
    return jax.shard_map(
        per_device,
        mesh=mesh,
        in_specs=placed,
        out_specs=(P(None, "fsdp", "tp", None), P(None, "fsdp", "tp", None)),
        check_vma=False,
    )
```

```python
import jax
import jax.numpy as jnp
from jax import lax
from jax.experimental import pallas as pl
from jax.experimental.pallas import tpu as pltpu
from jax.sharding import PartitionSpec as P

MESH = pl.DeviceIdType.MESH
BF16 = jnp.bfloat16
F32 = jnp.float32

LANES = 128
D = 7168
QR = 1536
KVR = 512
QK_NOPE = 128
V_DIM = 128
LAYERS = 2
HEADS = 128
FSDP = 32
TP = 8
PER_GROUP = HEADS // FSDP
RANKS = FSDP * TP
Q_ROWS = QR * QK_NOPE // RANKS // LANES
KV_ROWS = QK_NOPE * KVR // RANKS // LANES
O_ROWS = D * V_DIM // RANKS // LANES
SHARD_ROWS = HEADS * (Q_ROWS + 2 * KV_ROWS + O_ROWS)
CHUNKS = LAYERS * PER_GROUP
QUARTER = FSDP // TP
PAD = 16
LOADS = 4
ROWS_O = D // TP
ROWS_Q = QR // TP
HALF = FSDP // 2
STEPS = TP // 2
QUERY, KEY, VALUE, OUT = range(4)


def refresh_kernel(slices, owner, offs, x_hbm, q_ref, o_ref, k_ref, v_ref, *scratch):
    scratch = list(scratch)

    def take(n):
        out = scratch[:n]
        del scratch[:n]
        return out

    make_chunk = take(CHUNKS)
    land_chunk = take(CHUNKS)
    send_rows = take(CHUNKS)
    got_rows = take(CHUNKS)
    (
        make_small,
        land_small,
        make_kv,
        line_kv,
        plane_kv,
        got_kv,
        send_rest,
        got_rest,
        x_buf,
        flat,
        table,
        starts,
        o_wide,
        q_wide,
        kv_wide,
        kv_out,
    ) = take(16)
    (
        load_sem, table_sem, chunk_sent, chunk_here, rows_sent, rows_here, small_sent, small_here,
        rest_sent, rest_here, plane_sent, plane_here, ring_sent, ring_here, own_here,
    ) = take(len(scratch))

    f = lax.axis_index("fsdp")
    t = lax.axis_index("tp")

    load_rows = LAYERS * SHARD_ROWS // LOADS

    def load(i):
        part = pl.ds(i * load_rows, load_rows)
        return pltpu.make_async_copy(x_hbm.at[part], x_buf.at[part], load_sem.at[i])

    for i in range(LOADS):
        load(i).start()

    barrier = pltpu.get_barrier_semaphore()

    def greet_plane(d, carry):
        pl.semaphore_signal(barrier, inc=1, device_id=(lax.rem(f + d, FSDP), t), device_id_type=MESH)
        return carry

    def greet_line(d, carry):
        pl.semaphore_signal(barrier, inc=1, device_id=(f, lax.rem(t + d, TP)), device_id_type=MESH)
        return carry

    lax.fori_loop(1, TP, greet_line, 0)
    lax.fori_loop(1, FSDP, greet_plane, 0)

    square = (HEADS, HEADS)
    down_index = lax.broadcasted_iota(jnp.int32, square, 0)
    across_index = lax.broadcasted_iota(jnp.int32, square, 1)
    for l in range(LAYERS):

        def across(row):
            return jnp.broadcast_to(row, square)

        def down(row):
            return across(row).T

        owns = owner[pl.ds(l, 1), :]
        earlier = jnp.logical_and(across(owns) == down(owns), down_index < across_index)
        slot = owns * PER_GROUP + jnp.sum(earlier.astype(jnp.int32), axis=0, keepdims=True)
        hit = down(slot) == across_index
        for kind in range(4):
            begin = jnp.sum(jnp.where(hit, down(offs[l, pl.ds(kind, 1), :]), 0), axis=0, keepdims=True)
            table[pl.ds(4 * l + kind, 1), :] = PAD + l + 2 * (begin >> 7)
    fetch = pltpu.make_async_copy(table, starts, table_sem)
    fetch.start()

    flat[pl.ds(0, PAD), :] = jnp.zeros((PAD, LANES), F32)
    flat[pl.ds(PAD + LAYERS * SHARD_ROWS, PAD), :] = jnp.zeros((PAD, LANES), F32)
    block = 304
    for i in range(LOADS):
        load(i).wait()

        def widen(n, carry, i=i):
            at = pl.multiple_of(i * load_rows + n * block, 16)
            flat[pl.ds(PAD + at, block), :] = x_buf[pl.ds(at, block), :].astype(F32)
            return carry

        lax.fori_loop(0, load_rows // block, widen, 0)
    fetch.wait()

    place = lax.broadcasted_iota(jnp.int32, (8, LANES), 0)

    def pick(l, kind, g, first):
        return flat[pl.ds(starts[4 * l + kind, g] + 2 * first, 8, stride=2), :]

    def last_query_rows(l, to):
        tile = pick(l, QUERY, to * PER_GROUP, 4)
        for j in range(1, PER_GROUP):
            tile = jnp.where(place < 2 * j, tile, pick(l, QUERY, to * PER_GROUP + j, 4 - 2 * j))
        return tile.astype(BF16)

    def key_value_rows(l, to, pair):
        tile = None
        for j in range(2):
            g = to * PER_GROUP + 2 * pair + j
            key = pick(l, KEY, g, -4 * j)
            tile = key if tile is None else jnp.where(place < 4 * j, tile, key)
            tile = jnp.where(place < 4 * j + 2, tile, pick(l, VALUE, g, -4 * j - 2))
        return tile.astype(BF16)

    def gather_kv(to, carry):
        for pair in range(2):
            make_kv[to, pair] = key_value_rows(0, to, pair)
        return carry

    def gather_small(to, carry):
        for l in range(LAYERS):
            make_small[to, l] = last_query_rows(l, to)
        for pair in range(2):
            make_small[to, 2 + pair] = key_value_rows(1, to, pair)
        return carry

    def gather_chunk(c):
        l, j = c // PER_GROUP, c % PER_GROUP

        def one(to, carry):
            g = to * PER_GROUP + j
            for i in range(3):
                make_chunk[c][to, i] = pick(l, OUT, g, 8 * i).astype(BF16)
            make_chunk[c][to, 3] = jnp.where(place < 4, pick(l, OUT, g, 24), pick(l, QUERY, g, -4)).astype(BF16)
            return carry

        lax.fori_loop(0, FSDP, one, 0, unroll=2)

    def remote(src, dst, send_sem, recv_sem, device):
        return pltpu.make_async_remote_copy(
            src_ref=src, dst_ref=dst, send_sem=send_sem, recv_sem=recv_sem, device_id=device, device_id_type=MESH
        )

    def spread_plane(src, dst, send_sem, recv_sem):
        pltpu.make_async_copy(src.at[f], dst.at[f], recv_sem).start()

        def one(d, carry):
            to = lax.rem(f + d, FSDP)
            remote(src.at[to], dst.at[f], send_sem, recv_sem, (to, t)).start()
            return carry

        lax.fori_loop(1, FSDP, one, 0)

    def spread_line(src, dst, send_sem, recv_sem):
        for d in (4, 1, 7, 2, 6, 3, 5):
            to = lax.rem(t + d, TP)
            remote(src.at[to], dst.at[t], send_sem, recv_sem, (f, to)).start()
        pltpu.make_async_copy(src.at[t], dst.at[t], recv_sem).start()

    def all_arrived(dst, recv_sem):
        pltpu.make_async_copy(dst, dst, recv_sem).wait()

    def all_left(src, n, send_sem):
        pltpu.make_async_copy(src.at[pl.ds(0, n)], src.at[pl.ds(0, n)], send_sem).wait()

    def send_chunk(c):
        spread_plane(make_chunk[c], land_chunk[c], chunk_sent.at[c], chunk_here.at[c])

    def forward_rows(c):
        all_arrived(land_chunk[c], chunk_here.at[c])

        def one(to, carry):
            first = slices[to, f] * QUARTER
            for q in range(QUARTER):
                send_rows[c][to, pl.ds(4 * q, 4)] = land_chunk[c][first + q]
            return carry

        lax.fori_loop(0, TP, one, 0)
        spread_line(send_rows[c], got_rows[c], rows_sent.at[c], rows_here.at[c])

    def forward_rest():
        def one(to, carry):
            first = slices[to, f] * QUARTER
            for q in range(QUARTER):
                send_rest[to, q] = land_small[first + q, pl.ds(0, 2)]
            return carry

        lax.fori_loop(0, TP, one, 0)
        spread_line(send_rest, got_rest, rest_sent.at[0], rest_here.at[0])

    up = lax.rem(t + 1, TP)
    down_to = lax.rem(t + TP - 1, TP)
    ring_own = (make_kv, land_small.at[:, pl.ds(2, 2)])
    ring_got = (line_kv, got_kv)

    def ring_copy(l, direction, step):
        origin = lax.rem(t + (TP - step if direction == 0 else step), TP)
        if step == STEPS - 1:
            part = pl.ds(0, HALF) if direction == 0 else pl.ds(HALF, HALF)
        else:
            part = pl.ds(0, FSDP)
        dst = ring_got[l].at[origin, part]
        src = dst
        if step == 0:
            src = make_kv.at[part] if l == 0 else land_small.at[part, pl.ds(2, 2)]
        to = up if direction == 0 else down_to
        return remote(src, dst, ring_sent.at[l, direction, step], ring_here.at[l, direction, step], (f, to))

    def ring_own_copy(l):
        return pltpu.make_async_copy(ring_own[l], ring_got[l].at[t], own_here.at[l])

    def ring_start(l, step):
        for direction in range(2):
            if step:
                ring_copy(l, direction, step - 1).wait_recv()
            ring_copy(l, direction, step).start()
        if step == 0:
            ring_own_copy(l).start()

    def ring_end(l):
        for direction in range(2):
            ring_copy(l, direction, STEPS - 1).wait_recv()
        ring_own_copy(l).wait()

    def spread_kv():
        pltpu.make_async_copy(line_kv.at[:, f], plane_kv.at[f], plane_here.at[0]).start()

        def one(d, carry):
            to = lax.rem(f + d, FSDP)
            remote(line_kv.at[:, to], plane_kv.at[f], plane_sent.at[0], plane_here.at[0], (to, t)).start()
            return carry

        lax.fori_loop(1, FSDP, one, 0)

    def assemble_kv(l):
        src = plane_kv if l == 0 else got_kv
        inner = src.shape[1]
        f_step, t_step = (TP, 1) if l == 0 else (1, FSDP)

        def widen(i, carry):
            rows = pl.ds(pl.multiple_of(i * 16, 16), 16)
            kv_wide[rows, :] = src[i // inner, i % inner].astype(F32).reshape(16, LANES)
            return carry

        lax.fori_loop(0, TP * FSDP, widen, 0, unroll=4)

        def one_head(j, carry):
            for which, out_ref in ((0, k_ref), (1, v_ref)):
                for b in range(4):
                    for u in range(4):
                        first = (2 * u + b // 2) * t_step * 16 + 4 * j + 2 * which + b % 2
                        kv_out[pl.ds(u, FSDP, stride=4), :] = kv_wide[pl.ds(first, FSDP, stride=16 * f_step), :]
                    out_ref[l, j, :, pl.ds(b * LANES, LANES)] = kv_out[...].astype(BF16)
            return carry

        lax.fori_loop(0, PER_GROUP, one_head, 0)

    def assemble_rows(c):
        l, j = c // PER_GROUP, c % PER_GROUP
        all_arrived(got_rows[c], rows_here.at[c])

        def one(ti, carry):
            for q in range(QUARTER):
                block = got_rows[c][ti, pl.ds(4 * q, 4)].astype(F32).reshape(32, LANES)
                o_wide[pl.ds(q * TP * O_ROWS + ti * O_ROWS, O_ROWS), :] = block[:O_ROWS]
                q_wide[pl.ds(q * TP * Q_ROWS + ti * Q_ROWS, 4), :] = block[O_ROWS:]
                rest = got_rest[ti, q, l].astype(F32)
                q_wide[pl.ds(q * TP * Q_ROWS + ti * Q_ROWS + 4, 2), :] = rest[2 * j : 2 * j + 2]
            return carry

        lax.fori_loop(0, TP, one, 0)
        o_ref[l, j] = o_wide[...].astype(BF16)
        q_ref[l, j] = q_wide[...].astype(BF16)

    lax.fori_loop(0, FSDP, gather_kv, 0, unroll=2)
    pl.semaphore_wait(barrier, FSDP - 1 + TP - 1)
    ring_start(0, 0)
    lax.fori_loop(0, FSDP, gather_small, 0)
    spread_plane(make_small, land_small, small_sent.at[0], small_here.at[0])
    ahead = 2
    for c in range(ahead):
        gather_chunk(c)
        send_chunk(c)
    ring_start(0, 1)
    all_arrived(land_small, small_here.at[0])
    ring_start(1, 0)
    forward_rest()
    for c in range(CHUNKS):
        if c + ahead < CHUNKS:
            gather_chunk(c + ahead)
            send_chunk(c + ahead)
        forward_rows(c)
        if c == 0:
            all_arrived(got_rest, rest_here.at[0])
            ring_start(0, 2)
        elif c == 1:
            ring_start(1, 1)
            ring_start(0, 3)
        elif c == 2:
            ring_end(0)
            spread_kv()
            ring_start(1, 2)
        elif c == 3:
            ring_start(1, 3)
        elif c == 4:
            all_arrived(plane_kv, plane_here.at[0])
            assemble_kv(0)
        elif c == 5:
            ring_end(1)
            assemble_kv(1)
        if c >= 2:
            assemble_rows(c - 2)
    assemble_rows(CHUNKS - 2)
    assemble_rows(CHUNKS - 1)

    for c in range(CHUNKS):
        all_left(land_chunk[c], FSDP - 1, chunk_sent.at[c])
        all_left(send_rows[c], TP - 1, rows_sent.at[c])
    all_left(land_small, FSDP - 1, small_sent.at[0])
    all_left(plane_kv, FSDP - 1, plane_sent.at[0])
    all_left(send_rest, TP - 1, rest_sent.at[0])
    for l in range(LAYERS):
        for direction in range(2):
            for step in range(STEPS):
                ring_copy(l, direction, step).wait_send()


def collect(learner_flat, param_offsets, owner_map, slice_map):
    x = learner_flat.reshape(LAYERS, SHARD_ROWS, LANES).transpose(1, 0, 2).reshape(LAYERS * SHARD_ROWS, LANES)
    vmem = pl.BlockSpec(memory_space=pltpu.VMEM)
    dma = pltpu.SemaphoreType.DMA
    ring = (LAYERS, 2, STEPS)
    chunk = pltpu.VMEM((FSDP, 4, 8, LANES), BF16)
    rows = pltpu.VMEM((TP, 4 * QUARTER, 8, LANES), BF16)
    rest = pltpu.VMEM((TP, QUARTER, 2, 8, LANES), BF16)
    by_line = pltpu.VMEM((TP, FSDP, 2, 8, LANES), BF16)
    return pl.pallas_call(
        refresh_kernel,
        out_shape=(
            jax.ShapeDtypeStruct((LAYERS, PER_GROUP, ROWS_Q, LANES), BF16),
            jax.ShapeDtypeStruct((LAYERS, PER_GROUP, ROWS_O, LANES), BF16),
            jax.ShapeDtypeStruct((LAYERS, PER_GROUP, QK_NOPE, KVR), BF16),
            jax.ShapeDtypeStruct((LAYERS, PER_GROUP, V_DIM, KVR), BF16),
        ),
        in_specs=[pl.BlockSpec(memory_space=pltpu.SMEM), vmem, vmem, pl.BlockSpec(memory_space=pltpu.HBM)],
        out_specs=(vmem,) * 4,
        scratch_shapes=[chunk] * (2 * CHUNKS)
        + [rows] * (2 * CHUNKS)
        + [
            chunk,
            chunk,
            pltpu.VMEM((FSDP, 2, 8, LANES), BF16),
            by_line,
            pltpu.VMEM((FSDP, TP, 2, 8, LANES), BF16),
            by_line,
            rest,
            rest,
            pltpu.VMEM((LAYERS * SHARD_ROWS, LANES), BF16),
            pltpu.VMEM((LAYERS * SHARD_ROWS + 2 * PAD, LANES), F32),
            pltpu.VMEM((LAYERS * 4, HEADS), jnp.int32),
            pltpu.SMEM((LAYERS * 4, HEADS), jnp.int32),
            pltpu.VMEM((ROWS_O, LANES), F32),
            pltpu.VMEM((ROWS_Q, LANES), F32),
            pltpu.VMEM((TP * FSDP * 16, LANES), F32),
            pltpu.VMEM((QK_NOPE, LANES), F32),
            dma((LOADS,)), dma, dma((CHUNKS,)), dma((CHUNKS,)), dma((CHUNKS,)), dma((CHUNKS,)), dma((1,)), dma((1,)),
            dma((1,)), dma((1,)), dma((1,)), dma((1,)), dma(ring), dma(ring), dma((LAYERS,)),
        ],
        compiler_params=pltpu.CompilerParams(collective_id=0, has_side_effects=True, vmem_limit_bytes=32 << 20),
    )(*(pltpu.with_memory_space_constraint(a, pltpu.HBM) for a in (slice_map.T, owner_map, param_offsets.transpose(0, 2, 1), x)))


def product_kernel(q_ref, o_ref, k_ref, v_ref, q_out, o_out, q_buf, o_buf, q_sem, o_sem):
    def leave(i):
        l, j, at = i // PER_GROUP, i % PER_GROUP, i % 2
        return (
            pltpu.make_async_copy(o_buf.at[at], o_out.at[l, j], o_sem.at[at]),
            pltpu.make_async_copy(q_buf.at[at], q_out.at[l, j], q_sem.at[at]),
        )

    for i in range(CHUNKS):
        l, j, at = i // PER_GROUP, i % PER_GROUP, i % 2
        o_copy, q_copy = leave(i)
        if i >= 2:
            for copy in leave(i - 2):
                copy.wait()
        o_buf[at] = jnp.dot(o_ref[l, j], v_ref[l, j], preferred_element_type=F32).astype(BF16)
        o_copy.start()
        q_buf[at] = jnp.dot(q_ref[l, j], k_ref[l, j], preferred_element_type=F32).astype(BF16)
        q_copy.start()
    for i in range(CHUNKS - 2, CHUNKS):
        for copy in leave(i):
            copy.wait()


def products(query, out, key, value):
    vmem = pl.BlockSpec(memory_space=pltpu.VMEM)
    hbm = pl.BlockSpec(memory_space=pltpu.HBM)
    return pl.pallas_call(
        product_kernel,
        out_shape=(
            jax.ShapeDtypeStruct((LAYERS, PER_GROUP, ROWS_Q, KVR), BF16),
            jax.ShapeDtypeStruct((LAYERS, PER_GROUP, ROWS_O, KVR), BF16),
        ),
        in_specs=[vmem] * 4,
        out_specs=(hbm, hbm),
        scratch_shapes=[
            pltpu.VMEM((2, ROWS_Q, KVR), BF16),
            pltpu.VMEM((2, ROWS_O, KVR), BF16),
            pltpu.SemaphoreType.DMA((2,)),
            pltpu.SemaphoreType.DMA((2,)),
        ],
        compiler_params=pltpu.CompilerParams(vmem_limit_bytes=4 << 20),
    )(query, out, key, value)


def per_device(learner_flat, param_offsets, owner_map, slice_map):
    return products(*collect(learner_flat, param_offsets, owner_map, slice_map))


def solution(mesh):
    placed = (P(None, ("fsdp", "tp")), P(), P(), P())
    return jax.shard_map(
        per_device,
        mesh=mesh,
        in_specs=placed,
        out_specs=(P(None, "fsdp", "tp", None), P(None, "fsdp", "tp", None)),
        check_vma=False,
    )
```

```python
import jax
import jax.numpy as jnp
from jax import lax
from jax.experimental import pallas as pl
from jax.experimental.pallas import tpu as pltpu
from jax.sharding import PartitionSpec as P

MESH = pl.DeviceIdType.MESH
BF16 = jnp.bfloat16
F32 = jnp.float32

LANES = 128
D = 7168
QR = 1536
KVR = 512
QK_NOPE = 128
V_DIM = 128
LAYERS = 2
HEADS = 128
FSDP = 32
TP = 8
PER_GROUP = HEADS // FSDP
RANKS = FSDP * TP
Q_ROWS = QR * QK_NOPE // RANKS // LANES
KV_ROWS = QK_NOPE * KVR // RANKS // LANES
O_ROWS = D * V_DIM // RANKS // LANES
SHARD_ROWS = HEADS * (Q_ROWS + 2 * KV_ROWS + O_ROWS)
CHUNKS = LAYERS * PER_GROUP
QUARTER = FSDP // TP
PAD = 16
LOADS = 4
ROWS_O = D // TP
ROWS_Q = QR // TP
HALF = FSDP // 2
STEPS = TP // 2
QUERY, KEY, VALUE, OUT = range(4)


def refresh_kernel(slices, owner, offs, x_hbm, q_ref, o_ref, k_ref, v_ref, *scratch):
    scratch = list(scratch)

    def take(n):
        out = scratch[:n]
        del scratch[:n]
        return out

    make_chunk = take(CHUNKS)
    land_chunk = take(CHUNKS)
    send_rows = take(CHUNKS)
    got_rows = take(CHUNKS)
    (
        make_small,
        land_small,
        make_kv,
        line_kv,
        plane_kv,
        got_kv,
        send_rest,
        got_rest,
        x_buf,
        flat,
        table,
        starts,
        o_wide,
        q_wide,
        kv_wide,
        kv_out,
    ) = take(16)
    (
        load_sem, table_sem, chunk_sent, chunk_here, rows_sent, rows_here, small_sent, small_here,
        rest_sent, rest_here, plane_sent, plane_here, ring_sent, ring_here, own_here, line_sem,
    ) = take(len(scratch))

    f = lax.axis_index("fsdp")
    t = lax.axis_index("tp")

    load_rows = LAYERS * SHARD_ROWS // LOADS

    def load(i):
        part = pl.ds(i * load_rows, load_rows)
        return pltpu.make_async_copy(x_hbm.at[part], x_buf.at[part], load_sem.at[i])

    for i in range(LOADS):
        load(i).start()

    barrier = pltpu.get_barrier_semaphore()

    def greet_plane(d, carry):
        pl.semaphore_signal(barrier, inc=1, device_id=(lax.rem(f + d, FSDP), t), device_id_type=MESH)
        return carry

    up = lax.rem(t + 1, TP)
    down_to = lax.rem(t + TP - 1, TP)

    def tell_line(sem):
        for to in (up, down_to):
            pl.semaphore_signal(sem, inc=1, device_id=(f, to), device_id_type=MESH)

    def line_round(step):
        pl.semaphore_wait(line_sem.at[step], 2)
        if step + 1 < STEPS - 1:
            tell_line(line_sem.at[step + 1])

    tell_line(barrier)
    lax.fori_loop(1, FSDP, greet_plane, 0)

    square = (HEADS, HEADS)
    down_index = lax.broadcasted_iota(jnp.int32, square, 0)
    across_index = lax.broadcasted_iota(jnp.int32, square, 1)
    for l in range(LAYERS):

        def across(row):
            return jnp.broadcast_to(row, square)

        def down(row):
            return across(row).T

        owns = owner[pl.ds(l, 1), :]
        earlier = jnp.logical_and(across(owns) == down(owns), down_index < across_index)
        slot = owns * PER_GROUP + jnp.sum(earlier.astype(jnp.int32), axis=0, keepdims=True)
        hit = down(slot) == across_index
        for kind in range(4):
            begin = jnp.sum(jnp.where(hit, down(offs[l, pl.ds(kind, 1), :]), 0), axis=0, keepdims=True)
            table[pl.ds(4 * l + kind, 1), :] = PAD + l + 2 * (begin >> 7)
    fetch = pltpu.make_async_copy(table, starts, table_sem)
    fetch.start()

    flat[pl.ds(0, PAD), :] = jnp.zeros((PAD, LANES), F32)
    flat[pl.ds(PAD + LAYERS * SHARD_ROWS, PAD), :] = jnp.zeros((PAD, LANES), F32)
    block = 304
    for i in range(LOADS):
        load(i).wait()

        def widen(n, carry, i=i):
            at = pl.multiple_of(i * load_rows + n * block, 16)
            flat[pl.ds(PAD + at, block), :] = x_buf[pl.ds(at, block), :].astype(F32)
            return carry

        lax.fori_loop(0, load_rows // block, widen, 0)
    fetch.wait()

    place = lax.broadcasted_iota(jnp.int32, (8, LANES), 0)

    def pick(l, kind, g, first):
        return flat[pl.ds(starts[4 * l + kind, g] + 2 * first, 8, stride=2), :]

    def last_query_rows(l, to):
        tile = pick(l, QUERY, to * PER_GROUP, 4)
        for j in range(1, PER_GROUP):
            tile = jnp.where(place < 2 * j, tile, pick(l, QUERY, to * PER_GROUP + j, 4 - 2 * j))
        return tile.astype(BF16)

    def key_value_rows(l, to, pair):
        tile = None
        for j in range(2):
            g = to * PER_GROUP + 2 * pair + j
            key = pick(l, KEY, g, -4 * j)
            tile = key if tile is None else jnp.where(place < 4 * j, tile, key)
            tile = jnp.where(place < 4 * j + 2, tile, pick(l, VALUE, g, -4 * j - 2))
        return tile.astype(BF16)

    def gather_kv(to, carry):
        for pair in range(2):
            make_kv[to, pair] = key_value_rows(0, to, pair)
        return carry

    def gather_small(to, carry):
        for l in range(LAYERS):
            make_small[to, l] = last_query_rows(l, to)
        for pair in range(2):
            make_small[to, 2 + pair] = key_value_rows(1, to, pair)
        return carry

    def gather_chunk(c):
        l, j = c // PER_GROUP, c % PER_GROUP

        def one(to, carry):
            g = to * PER_GROUP + j
            for i in range(3):
                make_chunk[c][to, i] = pick(l, OUT, g, 8 * i).astype(BF16)
            make_chunk[c][to, 3] = jnp.where(place < 4, pick(l, OUT, g, 24), pick(l, QUERY, g, -4)).astype(BF16)
            return carry

        lax.fori_loop(0, FSDP, one, 0, unroll=2)

    def remote(src, dst, send_sem, recv_sem, device):
        return pltpu.make_async_remote_copy(
            src_ref=src, dst_ref=dst, send_sem=send_sem, recv_sem=recv_sem, device_id=device, device_id_type=MESH
        )

    def spread_plane(src, dst, send_sem, recv_sem):
        pltpu.make_async_copy(src.at[f], dst.at[f], recv_sem).start()

        def one(d, carry):
            to = lax.rem(f + d, FSDP)
            remote(src.at[to], dst.at[f], send_sem, recv_sem, (to, t)).start()
            return carry

        lax.fori_loop(1, FSDP, one, 0)

    def spread_line(src, dst, send_sem, recv_sem):
        for d in (1, 7, 2, 6, 3, 5, 4):
            to = lax.rem(t + d, TP)
            remote(src.at[to], dst.at[t], send_sem, recv_sem, (f, to)).start()
        pltpu.make_async_copy(src.at[t], dst.at[t], recv_sem).start()

    def all_arrived(dst, recv_sem):
        pltpu.make_async_copy(dst, dst, recv_sem).wait()

    def all_left(src, n, send_sem):
        pltpu.make_async_copy(src.at[pl.ds(0, n)], src.at[pl.ds(0, n)], send_sem).wait()

    def send_chunk(c):
        spread_plane(make_chunk[c], land_chunk[c], chunk_sent.at[c], chunk_here.at[c])

    def forward_rows(c):
        all_arrived(land_chunk[c], chunk_here.at[c])

        def one(to, carry):
            first = slices[to, f] * QUARTER
            for q in range(QUARTER):
                send_rows[c][to, pl.ds(4 * q, 4)] = land_chunk[c][first + q]
            return carry

        lax.fori_loop(0, TP, one, 0)
        spread_line(send_rows[c], got_rows[c], rows_sent.at[c], rows_here.at[c])

    def forward_rest():
        def one(to, carry):
            first = slices[to, f] * QUARTER
            for q in range(QUARTER):
                send_rest[to, q] = land_small[first + q, pl.ds(0, 2)]
            return carry

        lax.fori_loop(0, TP, one, 0)
        spread_line(send_rest, got_rest, rest_sent.at[0], rest_here.at[0])

    ring_own = (make_kv, land_small.at[:, pl.ds(2, 2)])
    ring_got = (line_kv, got_kv)

    def ring_copy(l, direction, step, half):
        origin = lax.rem(t + (TP - step if direction == 0 else step), TP)
        part = pl.ds(half * HALF, HALF)
        dst = ring_got[l].at[origin, part]
        src = dst
        if step == 0:
            src = make_kv.at[part] if l == 0 else land_small.at[part, pl.ds(2, 2)]
        to = up if direction == 0 else down_to
        at = (l, direction, step, half)
        return remote(src, dst, ring_sent.at[at], ring_here.at[at], (f, to))

    def ring_moves(step):
        return ((0, 0), (1, 1)) if step == STEPS - 1 else ((0, 0), (1, 0), (0, 1), (1, 1))

    def ring_own_copy(l):
        return pltpu.make_async_copy(ring_own[l], ring_got[l].at[t], own_here.at[l])

    def ring_start(l, step):
        for direction, half in ring_moves(step):
            if step:
                ring_copy(l, direction, step - 1, half).wait_recv()
            ring_copy(l, direction, step, half).start()
        if step == 0:
            ring_own_copy(l).start()

    def ring_end(l):
        for direction, half in ((0, 1), (1, 0)):
            ring_copy(l, direction, STEPS - 2, half).wait_recv()
        for direction, half in ring_moves(STEPS - 1):
            ring_copy(l, direction, STEPS - 1, half).wait_recv()
        ring_own_copy(l).wait()

    def spread_kv():
        pltpu.make_async_copy(line_kv.at[:, f], plane_kv.at[f], plane_here.at[0]).start()

        def one(d, carry):
            to = lax.rem(f + d, FSDP)
            remote(line_kv.at[:, to], plane_kv.at[f], plane_sent.at[0], plane_here.at[0], (to, t)).start()
            return carry

        lax.fori_loop(1, FSDP, one, 0)

    def assemble_kv(l):
        src = plane_kv if l == 0 else got_kv
        inner = src.shape[1]
        f_step, t_step = (TP, 1) if l == 0 else (1, FSDP)

        def widen(i, carry):
            rows = pl.ds(pl.multiple_of(i * 16, 16), 16)
            kv_wide[rows, :] = src[i // inner, i % inner].astype(F32).reshape(16, LANES)
            return carry

        lax.fori_loop(0, TP * FSDP, widen, 0, unroll=4)

        def one_head(j, carry):
            for which, out_ref in ((0, k_ref), (1, v_ref)):
                for b in range(4):
                    for u in range(4):
                        first = (2 * u + b // 2) * t_step * 16 + 4 * j + 2 * which + b % 2
                        kv_out[pl.ds(u, FSDP, stride=4), :] = kv_wide[pl.ds(first, FSDP, stride=16 * f_step), :]
                    out_ref[l, j, :, pl.ds(b * LANES, LANES)] = kv_out[...].astype(BF16)
            return carry

        lax.fori_loop(0, PER_GROUP, one_head, 0)

    def assemble_rows(c):
        l, j = c // PER_GROUP, c % PER_GROUP
        all_arrived(got_rows[c], rows_here.at[c])

        def one(ti, carry):
            for q in range(QUARTER):
                block = got_rows[c][ti, pl.ds(4 * q, 4)].astype(F32).reshape(32, LANES)
                o_wide[pl.ds(q * TP * O_ROWS + ti * O_ROWS, O_ROWS), :] = block[:O_ROWS]
                q_wide[pl.ds(q * TP * Q_ROWS + ti * Q_ROWS, 4), :] = block[O_ROWS:]
                rest = got_rest[ti, q, l].astype(F32)
                q_wide[pl.ds(q * TP * Q_ROWS + ti * Q_ROWS + 4, 2), :] = rest[2 * j : 2 * j + 2]
            return carry

        lax.fori_loop(0, TP, one, 0)
        o_ref[l, j] = o_wide[...].astype(BF16)
        q_ref[l, j] = q_wide[...].astype(BF16)

    lax.fori_loop(0, FSDP, gather_kv, 0, unroll=2)
    lax.fori_loop(0, FSDP, gather_small, 0)
    for c in range(CHUNKS):
        gather_chunk(c)
    pl.semaphore_wait(barrier, FSDP - 1 + 2)
    ring_start(0, 0)
    tell_line(line_sem.at[0])
    spread_plane(make_small, land_small, small_sent.at[0], small_here.at[0])
    send_chunk(0)
    line_round(0)
    ring_start(0, 1)
    send_chunk(1)
    line_round(1)
    all_arrived(land_small, small_here.at[0])
    ring_start(1, 0)
    line_round(2)
    forward_rest()
    for c in range(CHUNKS):
        if c < 3:
            send_chunk(2 * c + 2)
            send_chunk(2 * c + 3)
        forward_rows(c)
        if c == 0:
            ring_start(0, 2)
            ring_start(1, 1)
        elif c == 1:
            ring_start(0, 3)
            ring_start(1, 2)
        elif c == 2:
            ring_start(1, 3)
            ring_end(0)
            spread_kv()
        elif c == CHUNKS - 1:
            all_arrived(plane_kv, plane_here.at[0])
            assemble_kv(0)
            ring_end(1)
            assemble_kv(1)
        if c == 2:
            all_arrived(got_rest, rest_here.at[0])
        if c >= 2:
            assemble_rows(c - 2)
    assemble_rows(CHUNKS - 2)
    assemble_rows(CHUNKS - 1)

    for c in range(CHUNKS):
        all_left(land_chunk[c], FSDP - 1, chunk_sent.at[c])
        all_left(send_rows[c], TP - 1, rows_sent.at[c])
    all_left(land_small, FSDP - 1, small_sent.at[0])
    all_left(plane_kv, FSDP - 1, plane_sent.at[0])
    all_left(send_rest, TP - 1, rest_sent.at[0])
    for l in range(LAYERS):
        for direction in range(2):
            for step in range(STEPS):
                for half in range(2):
                    if (direction, half) in ring_moves(step):
                        ring_copy(l, direction, step, half).wait_send()


def collect(learner_flat, param_offsets, owner_map, slice_map):
    x = learner_flat.reshape(LAYERS, SHARD_ROWS, LANES).transpose(1, 0, 2).reshape(LAYERS * SHARD_ROWS, LANES)
    vmem = pl.BlockSpec(memory_space=pltpu.VMEM)
    dma = pltpu.SemaphoreType.DMA
    ring = (LAYERS, 2, STEPS, 2)
    chunk = pltpu.VMEM((FSDP, 4, 8, LANES), BF16)
    rows = pltpu.VMEM((TP, 4 * QUARTER, 8, LANES), BF16)
    rest = pltpu.VMEM((TP, QUARTER, 2, 8, LANES), BF16)
    by_line = pltpu.VMEM((TP, FSDP, 2, 8, LANES), BF16)
    return pl.pallas_call(
        refresh_kernel,
        out_shape=(
            jax.ShapeDtypeStruct((LAYERS, PER_GROUP, ROWS_Q, LANES), BF16),
            jax.ShapeDtypeStruct((LAYERS, PER_GROUP, ROWS_O, LANES), BF16),
            jax.ShapeDtypeStruct((LAYERS, PER_GROUP, QK_NOPE, KVR), BF16),
            jax.ShapeDtypeStruct((LAYERS, PER_GROUP, V_DIM, KVR), BF16),
        ),
        in_specs=[pl.BlockSpec(memory_space=pltpu.SMEM), vmem, vmem, pl.BlockSpec(memory_space=pltpu.HBM)],
        out_specs=(vmem,) * 4,
        scratch_shapes=[chunk] * (2 * CHUNKS)
        + [rows] * (2 * CHUNKS)
        + [
            chunk,
            chunk,
            pltpu.VMEM((FSDP, 2, 8, LANES), BF16),
            by_line,
            pltpu.VMEM((FSDP, TP, 2, 8, LANES), BF16),
            by_line,
            rest,
            rest,
            pltpu.VMEM((LAYERS * SHARD_ROWS, LANES), BF16),
            pltpu.VMEM((LAYERS * SHARD_ROWS + 2 * PAD, LANES), F32),
            pltpu.VMEM((LAYERS * 4, HEADS), jnp.int32),
            pltpu.SMEM((LAYERS * 4, HEADS), jnp.int32),
            pltpu.VMEM((ROWS_O, LANES), F32),
            pltpu.VMEM((ROWS_Q, LANES), F32),
            pltpu.VMEM((TP * FSDP * 16, LANES), F32),
            pltpu.VMEM((QK_NOPE, LANES), F32),
            dma((LOADS,)), dma, dma((CHUNKS,)), dma((CHUNKS,)), dma((CHUNKS,)), dma((CHUNKS,)), dma((1,)), dma((1,)),
            dma((1,)), dma((1,)), dma((1,)), dma((1,)), dma(ring), dma(ring), dma((LAYERS,)),
            pltpu.SemaphoreType.REGULAR((STEPS - 1,)),
        ],
        compiler_params=pltpu.CompilerParams(collective_id=0, has_side_effects=True, vmem_limit_bytes=32 << 20),
    )(*(pltpu.with_memory_space_constraint(a, pltpu.HBM) for a in (slice_map.T, owner_map, param_offsets.transpose(0, 2, 1), x)))


def product_kernel(q_ref, o_ref, k_ref, v_ref, q_out, o_out, q_buf, o_buf, q_sem, o_sem):
    def leave(i):
        l, j, at = i // PER_GROUP, i % PER_GROUP, i
        return (
            pltpu.make_async_copy(o_buf.at[at], o_out.at[l, j], o_sem.at[at]),
            pltpu.make_async_copy(q_buf.at[at], q_out.at[l, j], q_sem.at[at]),
        )

    for i in range(CHUNKS):
        l, j, at = i // PER_GROUP, i % PER_GROUP, i
        q_buf[at] = jnp.dot(q_ref[l, j], k_ref[l, j], preferred_element_type=F32).astype(BF16)
        pltpu.make_async_copy(q_buf.at[at], q_out.at[l, j], q_sem.at[at]).start()
        for r in range(0, ROWS_O, 224):
            o_buf[at, pl.ds(r, 224)] = jnp.dot(o_ref[l, j, pl.ds(r, 224)], v_ref[l, j], preferred_element_type=F32).astype(BF16)
            pltpu.make_async_copy(o_buf.at[at, pl.ds(r, 224)], o_out.at[l, j, pl.ds(r, 224)], o_sem.at[at]).start()
    for i in range(CHUNKS):
        for copy in leave(i):
            copy.wait()


def products(query, out, key, value):
    vmem = pl.BlockSpec(memory_space=pltpu.VMEM)
    hbm = pl.BlockSpec(memory_space=pltpu.HBM)
    return pl.pallas_call(
        product_kernel,
        out_shape=(
            jax.ShapeDtypeStruct((LAYERS, PER_GROUP, ROWS_Q, KVR), BF16),
            jax.ShapeDtypeStruct((LAYERS, PER_GROUP, ROWS_O, KVR), BF16),
        ),
        in_specs=[vmem] * 4,
        out_specs=(hbm, hbm),
        scratch_shapes=[
            pltpu.VMEM((CHUNKS, ROWS_Q, KVR), BF16),
            pltpu.VMEM((CHUNKS, ROWS_O, KVR), BF16),
            pltpu.SemaphoreType.DMA((CHUNKS,)),
            pltpu.SemaphoreType.DMA((CHUNKS,)),
        ],
        compiler_params=pltpu.CompilerParams(vmem_limit_bytes=12 << 20),
    )(query, out, key, value)


def per_device(learner_flat, param_offsets, owner_map, slice_map):
    return products(*collect(learner_flat, param_offsets, owner_map, slice_map))


def solution(mesh):
    placed = (P(None, ("fsdp", "tp")), P(), P(), P())
    return jax.shard_map(
        per_device,
        mesh=mesh,
        in_specs=placed,
        out_specs=(P(None, "fsdp", "tp", None), P(None, "fsdp", "tp", None)),
        check_vma=False,
    )
```

```python
import jax
import jax.numpy as jnp
from jax import lax
from jax.experimental import pallas as pl
from jax.experimental.pallas import tpu as pltpu
from jax.sharding import PartitionSpec as P

MESH = pl.DeviceIdType.MESH
BF16 = jnp.bfloat16
F32 = jnp.float32

LANES = 128
D = 7168
QR = 1536
KVR = 512
QK_NOPE = 128
V_DIM = 128
LAYERS = 2
HEADS = 128
FSDP = 32
TP = 8
PER_GROUP = HEADS // FSDP
RANKS = FSDP * TP
Q_ROWS = QR * QK_NOPE // RANKS // LANES
KV_ROWS = QK_NOPE * KVR // RANKS // LANES
O_ROWS = D * V_DIM // RANKS // LANES
SHARD_ROWS = HEADS * (Q_ROWS + 2 * KV_ROWS + O_ROWS)
CHUNKS = LAYERS * PER_GROUP
QUARTER = FSDP // TP
PAD = 16
LOADS = 4
ROWS_O = D // TP
ROWS_Q = QR // TP
HALF = FSDP // 2
STEPS = TP // 2
QUERY, KEY, VALUE, OUT = range(4)


def refresh_kernel(slices_hbm, owner_hbm, offs_hbm, x_hbm, q_ref, o_ref, k_ref, v_ref, *scratch):
    scratch = list(scratch)

    def take(n):
        out = scratch[:n]
        del scratch[:n]
        return out

    make_chunk = take(CHUNKS)
    land_chunk = take(CHUNKS)
    send_rows = take(CHUNKS)
    got_rows = take(CHUNKS)
    make_kv = take(LAYERS)
    line_kv = take(LAYERS)
    plane_kv = take(LAYERS)
    (
        make_small,
        land_small,
        send_rest,
        got_rest,
        x_buf,
        flat,
        table,
        starts,
        o_wide,
        q_wide,
        kv_wide,
        kv_out,
        slices,
        owner,
        offs,
    ) = take(15)
    (
        load_sem, table_sem, chunk_sent, chunk_here, rows_sent, rows_here, small_sent, small_here,
        rest_sent, rest_here, plane_sent, plane_here, ring_sent, ring_here, own_here, line_sem, map_sem,
    ) = take(len(scratch))

    f = lax.axis_index("fsdp")
    t = lax.axis_index("tp")

    load_rows = LAYERS * SHARD_ROWS // LOADS

    def load(i):
        part = pl.ds(i * load_rows, load_rows)
        return pltpu.make_async_copy(x_hbm.at[part], x_buf.at[part], load_sem.at[i])

    barrier = pltpu.get_barrier_semaphore()

    def greet_plane(d, carry):
        pl.semaphore_signal(barrier, inc=1, device_id=(lax.rem(f + d, FSDP), t), device_id_type=MESH)
        return carry

    up = lax.rem(t + 1, TP)
    down_to = lax.rem(t + TP - 1, TP)

    def tell_line(sem):
        for to in (up, down_to):
            pl.semaphore_signal(sem, inc=1, device_id=(f, to), device_id_type=MESH)

    def line_round(step):
        pl.semaphore_wait(line_sem.at[step], 2)
        if step + 1 < STEPS - 1:
            tell_line(line_sem.at[step + 1])

    tell_line(barrier)
    lax.fori_loop(1, FSDP, greet_plane, 0)
    maps = [
        pltpu.make_async_copy(src, dst, map_sem.at[i])
        for i, (src, dst) in enumerate(((owner_hbm, owner), (offs_hbm, offs), (slices_hbm, slices)))
    ]
    for copy in maps:
        copy.start()
    for i in range(LOADS):
        load(i).start()
    for copy in maps:
        copy.wait()

    square = (HEADS, HEADS)
    down_index = lax.broadcasted_iota(jnp.int32, square, 0)
    across_index = lax.broadcasted_iota(jnp.int32, square, 1)
    for l in range(LAYERS):

        def across(row):
            return jnp.broadcast_to(row, square)

        def down(row):
            return across(row).T

        owns = owner[pl.ds(l, 1), :]
        earlier = jnp.logical_and(across(owns) == down(owns), down_index < across_index)
        slot = owns * PER_GROUP + jnp.sum(earlier.astype(jnp.int32), axis=0, keepdims=True)
        hit = down(slot) == across_index
        for kind in range(4):
            begin = jnp.sum(jnp.where(hit, down(offs[l, pl.ds(kind, 1), :]), 0), axis=0, keepdims=True)
            table[pl.ds(4 * l + kind, 1), :] = PAD + l + 2 * (begin >> 7)
    fetch = pltpu.make_async_copy(table, starts, table_sem)
    fetch.start()

    flat[pl.ds(0, PAD), :] = jnp.zeros((PAD, LANES), F32)
    flat[pl.ds(PAD + LAYERS * SHARD_ROWS, PAD), :] = jnp.zeros((PAD, LANES), F32)
    block = 304
    for i in range(LOADS):
        load(i).wait()

        def widen(n, carry, i=i):
            at = pl.multiple_of(i * load_rows + n * block, 16)
            flat[pl.ds(PAD + at, block), :] = x_buf[pl.ds(at, block), :].astype(F32)
            return carry

        lax.fori_loop(0, load_rows // block, widen, 0)
    fetch.wait()

    place = lax.broadcasted_iota(jnp.int32, (8, LANES), 0)

    def pick(l, kind, g, first):
        return flat[pl.ds(starts[4 * l + kind, g] + 2 * first, 8, stride=2), :]

    def last_query_rows(l, to):
        tile = pick(l, QUERY, to * PER_GROUP, 4)
        for j in range(1, PER_GROUP):
            tile = jnp.where(place < 2 * j, tile, pick(l, QUERY, to * PER_GROUP + j, 4 - 2 * j))
        return tile.astype(BF16)

    def key_value_rows(l, to, pair):
        tile = None
        for j in range(2):
            g = to * PER_GROUP + 2 * pair + j
            key = pick(l, KEY, g, -4 * j)
            tile = key if tile is None else jnp.where(place < 4 * j, tile, key)
            tile = jnp.where(place < 4 * j + 2, tile, pick(l, VALUE, g, -4 * j - 2))
        return tile.astype(BF16)

    def gather_kv(l):
        def one(to, carry):
            for pair in range(2):
                make_kv[l][to, pair] = key_value_rows(l, to, pair)
            return carry

        lax.fori_loop(0, FSDP, one, 0, unroll=2)

    def gather_small(to, carry):
        for l in range(LAYERS):
            make_small[to, l] = last_query_rows(l, to)
        return carry

    def gather_chunk(c):
        l, j = c // PER_GROUP, c % PER_GROUP

        def one(to, carry):
            g = to * PER_GROUP + j
            for i in range(3):
                make_chunk[c][to, i] = pick(l, OUT, g, 8 * i).astype(BF16)
            make_chunk[c][to, 3] = jnp.where(place < 4, pick(l, OUT, g, 24), pick(l, QUERY, g, -4)).astype(BF16)
            return carry

        lax.fori_loop(0, FSDP, one, 0, unroll=2)

    def remote(src, dst, send_sem, recv_sem, device):
        return pltpu.make_async_remote_copy(
            src_ref=src, dst_ref=dst, send_sem=send_sem, recv_sem=recv_sem, device_id=device, device_id_type=MESH
        )

    def spread_plane(src, dst, send_sem, recv_sem):
        pltpu.make_async_copy(src.at[f], dst.at[f], recv_sem).start()

        def one(d, carry):
            to = lax.rem(f + d, FSDP)
            remote(src.at[to], dst.at[f], send_sem, recv_sem, (to, t)).start()
            return carry

        lax.fori_loop(1, FSDP, one, 0)

    def spread_line(src, dst, send_sem, recv_sem, order=(1, 7, 2, 6, 3, 5, 4)):
        for d in order:
            to = lax.rem(t + d, TP)
            remote(src.at[to], dst.at[t], send_sem, recv_sem, (f, to)).start()
        pltpu.make_async_copy(src.at[t], dst.at[t], recv_sem).start()

    def all_arrived(dst, recv_sem):
        pltpu.make_async_copy(dst, dst, recv_sem).wait()

    def all_left(src, n, send_sem):
        pltpu.make_async_copy(src.at[pl.ds(0, n)], src.at[pl.ds(0, n)], send_sem).wait()

    def send_chunk(c):
        spread_plane(make_chunk[c], land_chunk[c], chunk_sent.at[c], chunk_here.at[c])

    def forward_rows(c):
        all_arrived(land_chunk[c], chunk_here.at[c])

        def one(to, carry):
            first = slices[to, f] * QUARTER
            for q in range(QUARTER):
                send_rows[c][to, pl.ds(4 * q, 4)] = land_chunk[c][first + q]
            return carry

        lax.fori_loop(0, TP, one, 0)
        if c < CHUNKS - 1:
            spread_line(send_rows[c], got_rows[c], rows_sent.at[c], rows_here.at[c])
        else:
            spread_line(send_rows[c], got_rows[c], rows_sent.at[c], rows_here.at[c], (4, 3, 5, 2, 6, 1, 7))

    def forward_rest():
        def one(to, carry):
            first = slices[to, f] * QUARTER
            for q in range(QUARTER):
                send_rest[to, q] = land_small[first + q]
            return carry

        lax.fori_loop(0, TP, one, 0)
        spread_line(send_rest, got_rest, rest_sent.at[0], rest_here.at[0])

    def ring_copy(l, direction, step, half):
        origin = lax.rem(t + (TP - step if direction == 0 else step), TP)
        part = pl.ds(half * HALF, HALF)
        dst = line_kv[l].at[origin, part]
        src = make_kv[l].at[part] if step == 0 else dst
        to = up if direction == 0 else down_to
        at = (l, direction, step, half)
        return remote(src, dst, ring_sent.at[at], ring_here.at[at], (f, to))

    def ring_moves(step):
        return ((0, 0), (1, 1)) if step == STEPS - 1 else ((0, 0), (1, 0), (0, 1), (1, 1))

    def ring_own_copy(l):
        return pltpu.make_async_copy(make_kv[l], line_kv[l].at[t], own_here.at[l])

    def ring_start(l, step):
        for direction, half in ring_moves(step):
            if step:
                ring_copy(l, direction, step - 1, half).wait_recv()
            ring_copy(l, direction, step, half).start()
        if step == 0:
            ring_own_copy(l).start()

    def ring_end(l):
        for direction, half in ((0, 1), (1, 0)):
            ring_copy(l, direction, STEPS - 2, half).wait_recv()
        for direction, half in ring_moves(STEPS - 1):
            ring_copy(l, direction, STEPS - 1, half).wait_recv()
        ring_own_copy(l).wait()

    def spread_kv(l):
        pltpu.make_async_copy(line_kv[l].at[:, f], plane_kv[l].at[f], plane_here.at[l]).start()

        def one(d, carry):
            to = lax.rem(f + d, FSDP)
            remote(line_kv[l].at[:, to], plane_kv[l].at[f], plane_sent.at[l], plane_here.at[l], (to, t)).start()
            return carry

        lax.fori_loop(1, FSDP, one, 0)

    def assemble_kv(l):
        def widen(i, carry):
            rows = pl.ds(pl.multiple_of(i * 16, 16), 16)
            kv_wide[rows, :] = plane_kv[l][i // TP, i % TP].astype(F32).reshape(16, LANES)
            return carry

        lax.fori_loop(0, TP * FSDP, widen, 0, unroll=4)

        def one_head(j, carry):
            for which, out_ref in ((0, k_ref), (1, v_ref)):
                for b in range(4):
                    for u in range(4):
                        first = (2 * u + b // 2) * 16 + 4 * j + 2 * which + b % 2
                        kv_out[pl.ds(u, FSDP, stride=4), :] = kv_wide[pl.ds(first, FSDP, stride=16 * TP), :]
                    out_ref[l, j, :, pl.ds(b * LANES, LANES)] = kv_out[...].astype(BF16)
            return carry

        lax.fori_loop(0, PER_GROUP, one_head, 0)

    def assemble_rows(c):
        l, j = c // PER_GROUP, c % PER_GROUP
        all_arrived(got_rows[c], rows_here.at[c])

        def one(ti, carry):
            for q in range(QUARTER):
                block = got_rows[c][ti, pl.ds(4 * q, 4)].astype(F32).reshape(32, LANES)
                o_wide[pl.ds(q * TP * O_ROWS + ti * O_ROWS, O_ROWS), :] = block[:O_ROWS]
                q_wide[pl.ds(q * TP * Q_ROWS + ti * Q_ROWS, 4), :] = block[O_ROWS:]
                rest = got_rest[ti, q, l].astype(F32)
                q_wide[pl.ds(q * TP * Q_ROWS + ti * Q_ROWS + 4, 2), :] = rest[2 * j : 2 * j + 2]
            return carry

        lax.fori_loop(0, TP, one, 0)
        o_ref[l, j] = o_wide[...].astype(BF16)
        q_ref[l, j] = q_wide[...].astype(BF16)

    gather_kv(0)
    pl.semaphore_wait(barrier, FSDP - 1 + 2)
    ring_start(0, 0)
    tell_line(line_sem.at[0])
    gather_chunk(0)
    send_chunk(0)
    gather_kv(1)
    ring_start(1, 0)
    line_round(0)
    lax.fori_loop(0, FSDP, gather_small, 0)
    spread_plane(make_small, land_small, small_sent.at[0], small_here.at[0])
    gather_chunk(1)
    send_chunk(1)
    line_round(1)
    ring_start(0, 1)
    gather_chunk(2)
    gather_chunk(3)
    line_round(2)
    ring_start(1, 1)
    for c in range(CHUNKS):
        if c < 3:
            send_chunk(2 * c + 2)
            send_chunk(2 * c + 3)
        forward_rows(c)
        if c < 2:
            gather_chunk(2 * c + 4)
            gather_chunk(2 * c + 5)
        if c == 0:
            ring_start(0, 2)
            all_arrived(land_small, small_here.at[0])
            forward_rest()
            ring_start(1, 2)
        elif c == 1:
            ring_start(0, 3)
            ring_start(1, 3)
        elif c == 2:
            ring_end(0)
            spread_kv(0)
        elif c == 3:
            ring_end(1)
            spread_kv(1)
        elif c == CHUNKS - 1:
            for l in range(LAYERS):
                all_arrived(plane_kv[l], plane_here.at[l])
                assemble_kv(l)
        if c == 2:
            all_arrived(got_rest, rest_here.at[0])
        if c >= 2:
            assemble_rows(c - 2)
    assemble_rows(CHUNKS - 2)
    assemble_rows(CHUNKS - 1)

    for c in range(CHUNKS):
        all_left(land_chunk[c], FSDP - 1, chunk_sent.at[c])
        all_left(send_rows[c], TP - 1, rows_sent.at[c])
    all_left(land_small, FSDP - 1, small_sent.at[0])
    all_left(send_rest, TP - 1, rest_sent.at[0])
    for l in range(LAYERS):
        all_left(plane_kv[l], FSDP - 1, plane_sent.at[l])
        for direction in range(2):
            for step in range(STEPS):
                for half in range(2):
                    if (direction, half) in ring_moves(step):
                        ring_copy(l, direction, step, half).wait_send()


def collect(learner_flat, param_offsets, owner_map, slice_map):
    x = learner_flat.reshape(LAYERS, SHARD_ROWS, LANES).transpose(1, 0, 2).reshape(LAYERS * SHARD_ROWS, LANES)
    vmem = pl.BlockSpec(memory_space=pltpu.VMEM)
    dma = pltpu.SemaphoreType.DMA
    ring = (LAYERS, 2, STEPS, 2)
    chunk = pltpu.VMEM((FSDP, 4, 8, LANES), BF16)
    rows = pltpu.VMEM((TP, 4 * QUARTER, 8, LANES), BF16)
    rest = pltpu.VMEM((TP, QUARTER, 2, 8, LANES), BF16)
    return pl.pallas_call(
        refresh_kernel,
        out_shape=(
            jax.ShapeDtypeStruct((LAYERS, PER_GROUP, ROWS_Q, LANES), BF16),
            jax.ShapeDtypeStruct((LAYERS, PER_GROUP, ROWS_O, LANES), BF16),
            jax.ShapeDtypeStruct((LAYERS, PER_GROUP, QK_NOPE, KVR), BF16),
            jax.ShapeDtypeStruct((LAYERS, PER_GROUP, V_DIM, KVR), BF16),
        ),
        in_specs=[pl.BlockSpec(memory_space=pltpu.HBM)] * 4,
        out_specs=(vmem,) * 4,
        scratch_shapes=[chunk] * (2 * CHUNKS)
        + [rows] * (2 * CHUNKS)
        + [pltpu.VMEM((FSDP, 2, 8, LANES), BF16)] * LAYERS
        + [pltpu.VMEM((TP, FSDP, 2, 8, LANES), BF16)] * LAYERS
        + [pltpu.VMEM((FSDP, TP, 2, 8, LANES), BF16)] * LAYERS
        + [
            pltpu.VMEM((FSDP, LAYERS, 8, LANES), BF16),
            pltpu.VMEM((FSDP, LAYERS, 8, LANES), BF16),
            rest,
            rest,
            pltpu.VMEM((LAYERS * SHARD_ROWS, LANES), BF16),
            pltpu.VMEM((LAYERS * SHARD_ROWS + 2 * PAD, LANES), F32),
            pltpu.VMEM((LAYERS * 4, HEADS), jnp.int32),
            pltpu.SMEM((LAYERS * 4, HEADS), jnp.int32),
            pltpu.VMEM((ROWS_O, LANES), F32),
            pltpu.VMEM((ROWS_Q, LANES), F32),
            pltpu.VMEM((TP * FSDP * 16, LANES), F32),
            pltpu.VMEM((QK_NOPE, LANES), F32),
            pltpu.SMEM((TP, FSDP), jnp.int32),
            pltpu.VMEM((LAYERS, HEADS), jnp.int32),
            pltpu.VMEM((LAYERS, 4, HEADS), jnp.int32),
            dma((LOADS,)), dma, dma((CHUNKS,)), dma((CHUNKS,)), dma((CHUNKS,)), dma((CHUNKS,)), dma((1,)), dma((1,)),
            dma((1,)), dma((1,)), dma((LAYERS,)), dma((LAYERS,)), dma(ring), dma(ring), dma((LAYERS,)),
            pltpu.SemaphoreType.REGULAR((STEPS - 1,)), dma((3,)),
        ],
        compiler_params=pltpu.CompilerParams(collective_id=0, has_side_effects=True, vmem_limit_bytes=32 << 20),
    )(*(pltpu.with_memory_space_constraint(a, pltpu.HBM) for a in (slice_map.T, owner_map, param_offsets.transpose(0, 2, 1), x)))


def product_kernel(q_ref, o_ref, k_ref, v_ref, q_out, o_out, q_buf, o_buf, q_sem, o_sem):
    def leave(i):
        l, j, at = i // PER_GROUP, i % PER_GROUP, i
        return (
            pltpu.make_async_copy(o_buf.at[at], o_out.at[l, j], o_sem.at[at]),
            pltpu.make_async_copy(q_buf.at[at], q_out.at[l, j], q_sem.at[at]),
        )

    for i in range(CHUNKS):
        l, j, at = i // PER_GROUP, i % PER_GROUP, i
        q_buf[at] = jnp.dot(q_ref[l, j], k_ref[l, j], preferred_element_type=F32).astype(BF16)
        pltpu.make_async_copy(q_buf.at[at], q_out.at[l, j], q_sem.at[at]).start()
        for r in range(0, ROWS_O, 224):
            o_buf[at, pl.ds(r, 224)] = jnp.dot(o_ref[l, j, pl.ds(r, 224)], v_ref[l, j], preferred_element_type=F32).astype(BF16)
            pltpu.make_async_copy(o_buf.at[at, pl.ds(r, 224)], o_out.at[l, j, pl.ds(r, 224)], o_sem.at[at]).start()
    for i in range(CHUNKS):
        for copy in leave(i):
            copy.wait()


def products(query, out, key, value):
    vmem = pl.BlockSpec(memory_space=pltpu.VMEM)
    hbm = pl.BlockSpec(memory_space=pltpu.HBM)
    return pl.pallas_call(
        product_kernel,
        out_shape=(
            jax.ShapeDtypeStruct((LAYERS, PER_GROUP, ROWS_Q, KVR), BF16),
            jax.ShapeDtypeStruct((LAYERS, PER_GROUP, ROWS_O, KVR), BF16),
        ),
        in_specs=[vmem] * 4,
        out_specs=(hbm, hbm),
        scratch_shapes=[
            pltpu.VMEM((CHUNKS, ROWS_Q, KVR), BF16),
            pltpu.VMEM((CHUNKS, ROWS_O, KVR), BF16),
            pltpu.SemaphoreType.DMA((CHUNKS,)),
            pltpu.SemaphoreType.DMA((CHUNKS,)),
        ],
        compiler_params=pltpu.CompilerParams(vmem_limit_bytes=12 << 20),
    )(query, out, key, value)


def per_device(learner_flat, param_offsets, owner_map, slice_map):
    return products(*collect(learner_flat, param_offsets, owner_map, slice_map))


def solution(mesh):
    placed = (P(None, ("fsdp", "tp")), P(), P(), P())
    return jax.shard_map(
        per_device,
        mesh=mesh,
        in_specs=placed,
        out_specs=(P(None, "fsdp", "tp", None), P(None, "fsdp", "tp", None)),
        check_vma=False,
    )
```

```python
import jax
import jax.numpy as jnp
from jax import lax
from jax.experimental import pallas as pl
from jax.experimental.pallas import tpu as pltpu
from jax.sharding import PartitionSpec as P

MESH = pl.DeviceIdType.MESH
BF16 = jnp.bfloat16
F32 = jnp.float32

LANES = 128
D = 7168
QR = 1536
KVR = 512
QK_NOPE = 128
V_DIM = 128
LAYERS = 2
HEADS = 128
FSDP = 32
TP = 8
PER_GROUP = HEADS // FSDP
RANKS = FSDP * TP
Q_ROWS = QR * QK_NOPE // RANKS // LANES
KV_ROWS = QK_NOPE * KVR // RANKS // LANES
O_ROWS = D * V_DIM // RANKS // LANES
SHARD_ROWS = HEADS * (Q_ROWS + 2 * KV_ROWS + O_ROWS)
CHUNKS = LAYERS * PER_GROUP
QUARTER = FSDP // TP
PAD = 16
LOADS = 4
ROWS_O = D // TP
ROWS_Q = QR // TP
HALF = FSDP // 2
STEPS = TP // 2
QUERY, KEY, VALUE, OUT = range(4)


def refresh_kernel(slices_hbm, owner_hbm, offs_hbm, x_hbm, q_ref, o_ref, k_ref, v_ref, *scratch):
    scratch = list(scratch)

    def take(n):
        out = scratch[:n]
        del scratch[:n]
        return out

    make_chunk = take(CHUNKS)
    land_chunk = take(CHUNKS)
    send_rows = take(CHUNKS)
    got_rows = take(CHUNKS)
    make_kv = take(LAYERS)
    line_kv = take(LAYERS)
    plane_kv = take(LAYERS)
    (
        make_small,
        land_small,
        send_rest,
        got_rest,
        x_buf,
        flat,
        table,
        starts,
        o_wide,
        q_wide,
        kv_wide,
        kv_out,
        slices,
        owner,
        offs,
    ) = take(15)
    (
        load_sem, table_sem, chunk_sent, chunk_here, rows_sent, rows_here, small_sent, small_here,
        rest_sent, rest_here, plane_sent, plane_here, ring_sent, ring_here, own_here, line_sem, map_sem,
    ) = take(len(scratch))

    f = lax.axis_index("fsdp")
    t = lax.axis_index("tp")

    load_rows = LAYERS * SHARD_ROWS // LOADS

    def load(i):
        part = pl.ds(i * load_rows, load_rows)
        return pltpu.make_async_copy(x_hbm.at[part], x_buf.at[part], load_sem.at[i])

    barrier = pltpu.get_barrier_semaphore()

    def greet_plane(d, carry):
        pl.semaphore_signal(barrier, inc=1, device_id=(lax.rem(f + d, FSDP), t), device_id_type=MESH)
        return carry

    up = lax.rem(t + 1, TP)
    down_to = lax.rem(t + TP - 1, TP)

    def tell_line(sem):
        for to in (up, down_to):
            pl.semaphore_signal(sem, inc=1, device_id=(f, to), device_id_type=MESH)

    def line_round(step):
        pl.semaphore_wait(line_sem.at[step], 2)
        if step + 1 < STEPS - 1:
            tell_line(line_sem.at[step + 1])

    tell_line(barrier)
    lax.fori_loop(1, FSDP, greet_plane, 0)
    maps = [
        pltpu.make_async_copy(src, dst, map_sem.at[i])
        for i, (src, dst) in enumerate(((owner_hbm, owner), (offs_hbm, offs), (slices_hbm, slices)))
    ]
    for copy in maps:
        copy.start()
    for i in range(LOADS):
        load(i).start()
    for copy in maps:
        copy.wait()

    square = (HEADS, HEADS)
    down_index = lax.broadcasted_iota(jnp.int32, square, 0)
    across_index = lax.broadcasted_iota(jnp.int32, square, 1)
    for l in range(LAYERS):

        def across(row):
            return jnp.broadcast_to(row, square)

        def down(row):
            return across(row).T

        owns = owner[pl.ds(l, 1), :]
        earlier = jnp.logical_and(across(owns) == down(owns), down_index < across_index)
        slot = owns * PER_GROUP + jnp.sum(earlier.astype(jnp.int32), axis=0, keepdims=True)
        hit = down(slot) == across_index
        for kind in range(4):
            begin = jnp.sum(jnp.where(hit, down(offs[l, pl.ds(kind, 1), :]), 0), axis=0, keepdims=True)
            table[pl.ds(4 * l + kind, 1), :] = PAD + l + 2 * (begin >> 7)
    fetch = pltpu.make_async_copy(table, starts, table_sem)
    fetch.start()

    flat[pl.ds(0, PAD), :] = jnp.zeros((PAD, LANES), F32)
    flat[pl.ds(PAD + LAYERS * SHARD_ROWS, PAD), :] = jnp.zeros((PAD, LANES), F32)
    block = 304
    for i in range(LOADS):
        load(i).wait()

        def widen(n, carry, i=i):
            at = pl.multiple_of(i * load_rows + n * block, 16)
            flat[pl.ds(PAD + at, block), :] = x_buf[pl.ds(at, block), :].astype(F32)
            return carry

        lax.fori_loop(0, load_rows // block, widen, 0)
    fetch.wait()

    place = lax.broadcasted_iota(jnp.int32, (8, LANES), 0)

    def pick(l, kind, g, first):
        return flat[pl.ds(starts[4 * l + kind, g] + 2 * first, 8, stride=2), :]

    def last_query_rows(l, to):
        tile = pick(l, QUERY, to * PER_GROUP, 4)
        for j in range(1, PER_GROUP):
            tile = jnp.where(place < 2 * j, tile, pick(l, QUERY, to * PER_GROUP + j, 4 - 2 * j))
        return tile.astype(BF16)

    def key_value_rows(l, to, pair):
        tile = None
        for j in range(2):
            g = to * PER_GROUP + 2 * pair + j
            key = pick(l, KEY, g, -4 * j)
            tile = key if tile is None else jnp.where(place < 4 * j, tile, key)
            tile = jnp.where(place < 4 * j + 2, tile, pick(l, VALUE, g, -4 * j - 2))
        return tile.astype(BF16)

    def gather_kv(l):
        def one(to, carry):
            for pair in range(2):
                make_kv[l][to, pair] = key_value_rows(l, to, pair)
            return carry

        lax.fori_loop(0, FSDP, one, 0, unroll=2)

    def gather_small(to, carry):
        for l in range(LAYERS):
            make_small[to, l] = last_query_rows(l, to)
        return carry

    def gather_chunk(c):
        l, j = c // PER_GROUP, c % PER_GROUP

        def one(to, carry):
            g = to * PER_GROUP + j
            for i in range(3):
                make_chunk[c][to, i] = pick(l, OUT, g, 8 * i).astype(BF16)
            make_chunk[c][to, 3] = jnp.where(place < 4, pick(l, OUT, g, 24), pick(l, QUERY, g, -4)).astype(BF16)
            return carry

        lax.fori_loop(0, FSDP, one, 0, unroll=2)

    def remote(src, dst, send_sem, recv_sem, device):
        return pltpu.make_async_remote_copy(
            src_ref=src, dst_ref=dst, send_sem=send_sem, recv_sem=recv_sem, device_id=device, device_id_type=MESH
        )

    def spread_plane(src, dst, send_sem, recv_sem):
        pltpu.make_async_copy(src.at[f], dst.at[f], recv_sem).start()

        def one(d, carry):
            to = lax.rem(f + d, FSDP)
            remote(src.at[to], dst.at[f], send_sem, recv_sem, (to, t)).start()
            return carry

        lax.fori_loop(1, FSDP, one, 0)

    def spread_line(src, dst, send_sem, recv_sem, order=(1, 7, 2, 6, 3, 5, 4)):
        for d in order:
            to = lax.rem(t + d, TP)
            remote(src.at[to], dst.at[t], send_sem, recv_sem, (f, to)).start()
        pltpu.make_async_copy(src.at[t], dst.at[t], recv_sem).start()

    def all_arrived(dst, recv_sem):
        pltpu.make_async_copy(dst, dst, recv_sem).wait()

    def all_left(src, n, send_sem):
        pltpu.make_async_copy(src.at[pl.ds(0, n)], src.at[pl.ds(0, n)], send_sem).wait()

    def send_chunk(c):
        spread_plane(make_chunk[c], land_chunk[c], chunk_sent.at[c], chunk_here.at[c])

    def forward_rows(c):
        all_arrived(land_chunk[c], chunk_here.at[c])

        def one(to, carry):
            first = slices[to, f] * QUARTER
            for q in range(QUARTER):
                send_rows[c][to, pl.ds(4 * q, 4)] = land_chunk[c][first + q]
            return carry

        lax.fori_loop(0, TP, one, 0)
        if c < CHUNKS - 1:
            spread_line(send_rows[c], got_rows[c], rows_sent.at[c], rows_here.at[c])
        else:
            spread_line(send_rows[c], got_rows[c], rows_sent.at[c], rows_here.at[c], (4, 3, 5, 2, 6, 1, 7))

    def forward_rest():
        def one(to, carry):
            first = slices[to, f] * QUARTER
            for q in range(QUARTER):
                send_rest[to, q] = land_small[first + q]
            return carry

        lax.fori_loop(0, TP, one, 0)
        spread_line(send_rest, got_rest, rest_sent.at[0], rest_here.at[0])

    def ring_copy(l, direction, step, half):
        origin = lax.rem(t + (TP - step if direction == 0 else step), TP)
        part = pl.ds(half * HALF, HALF)
        dst = line_kv[l].at[origin, part]
        src = make_kv[l].at[part] if step == 0 else dst
        to = up if direction == 0 else down_to
        at = (l, direction, step, half)
        return remote(src, dst, ring_sent.at[at], ring_here.at[at], (f, to))

    def ring_moves(step):
        return ((0, 0), (1, 1)) if step == STEPS - 1 else ((0, 0), (1, 0), (0, 1), (1, 1))

    def ring_own_copy(l):
        return pltpu.make_async_copy(make_kv[l], line_kv[l].at[t], own_here.at[l])

    def ring_start(l, step):
        for direction, half in ring_moves(step):
            if step:
                ring_copy(l, direction, step - 1, half).wait_recv()
            ring_copy(l, direction, step, half).start()
        if step == 0:
            ring_own_copy(l).start()

    def ring_end(l):
        for direction, half in ((0, 1), (1, 0)):
            ring_copy(l, direction, STEPS - 2, half).wait_recv()
        for direction, half in ring_moves(STEPS - 1):
            ring_copy(l, direction, STEPS - 1, half).wait_recv()
        ring_own_copy(l).wait()

    def spread_kv(l):
        pltpu.make_async_copy(line_kv[l].at[:, f], plane_kv[l].at[f], plane_here.at[l]).start()

        def one(d, carry):
            to = lax.rem(f + d, FSDP)
            remote(line_kv[l].at[:, to], plane_kv[l].at[f], plane_sent.at[l], plane_here.at[l], (to, t)).start()
            return carry

        lax.fori_loop(1, FSDP, one, 0)

    def assemble_kv(l):
        def widen(i, carry):
            rows = pl.ds(pl.multiple_of(i * 16, 16), 16)
            kv_wide[rows, :] = plane_kv[l][i // TP, i % TP].astype(F32).reshape(16, LANES)
            return carry

        lax.fori_loop(0, TP * FSDP, widen, 0, unroll=4)

        def one_head(j, carry):
            for which, out_ref in ((0, k_ref), (1, v_ref)):
                for b in range(4):
                    for u in range(4):
                        first = (2 * u + b // 2) * 16 + 4 * j + 2 * which + b % 2
                        kv_out[pl.ds(u, FSDP, stride=4), :] = kv_wide[pl.ds(first, FSDP, stride=16 * TP), :]
                    out_ref[l, j, :, pl.ds(b * LANES, LANES)] = kv_out[pl.ds(0, QK_NOPE), :].astype(BF16)
            return carry

        lax.fori_loop(0, PER_GROUP, one_head, 0)

    def assemble_rows(c):
        l, j = c // PER_GROUP, c % PER_GROUP
        all_arrived(got_rows[c], rows_here.at[c])

        def one(ti, carry):
            for q in range(QUARTER):
                block = got_rows[c][ti, pl.ds(4 * q, 4)].astype(F32).reshape(32, LANES)
                o_wide[pl.ds(q * TP * O_ROWS + ti * O_ROWS, O_ROWS), :] = block[:O_ROWS]
                q_wide[pl.ds(q * TP * Q_ROWS + ti * Q_ROWS, 4), :] = block[O_ROWS:]
                rest = got_rest[ti, q, l].astype(F32)
                q_wide[pl.ds(q * TP * Q_ROWS + ti * Q_ROWS + 4, 2), :] = rest[2 * j : 2 * j + 2]
            return carry

        lax.fori_loop(0, TP, one, 0)
        o_ref[l, j] = o_wide[...].astype(BF16)
        q_ref[l, j] = q_wide[...].astype(BF16)

    gather_kv(0)
    pl.semaphore_wait(barrier, FSDP - 1 + 2)
    ring_start(0, 0)
    tell_line(line_sem.at[0])
    gather_chunk(0)
    send_chunk(0)
    gather_kv(1)
    ring_start(1, 0)
    line_round(0)
    lax.fori_loop(0, FSDP, gather_small, 0)
    spread_plane(make_small, land_small, small_sent.at[0], small_here.at[0])
    gather_chunk(1)
    send_chunk(1)
    line_round(1)
    ring_start(0, 1)
    gather_chunk(2)
    gather_chunk(3)
    line_round(2)
    ring_start(1, 1)
    for c in range(CHUNKS):
        if c < 3:
            send_chunk(2 * c + 2)
            send_chunk(2 * c + 3)
        forward_rows(c)
        if c < 2:
            gather_chunk(2 * c + 4)
            gather_chunk(2 * c + 5)
        if c == 0:
            ring_start(0, 2)
            all_arrived(land_small, small_here.at[0])
            forward_rest()
            ring_start(1, 2)
        elif c == 1:
            ring_start(0, 3)
            ring_start(1, 3)
        elif c == 2:
            ring_end(0)
            spread_kv(0)
        elif c == 3:
            ring_end(1)
            spread_kv(1)
        elif c == CHUNKS - 1:
            for l in range(LAYERS):
                all_arrived(plane_kv[l], plane_here.at[l])
                assemble_kv(l)
        if c == 2:
            all_arrived(got_rest, rest_here.at[0])
        if c >= 2:
            assemble_rows(c - 2)
    assemble_rows(CHUNKS - 2)
    assemble_rows(CHUNKS - 1)

    for c in range(CHUNKS):
        all_left(land_chunk[c], FSDP - 1, chunk_sent.at[c])
        all_left(send_rows[c], TP - 1, rows_sent.at[c])
    all_left(land_small, FSDP - 1, small_sent.at[0])
    all_left(send_rest, TP - 1, rest_sent.at[0])
    for l in range(LAYERS):
        all_left(plane_kv[l], FSDP - 1, plane_sent.at[l])
        for direction in range(2):
            for step in range(STEPS):
                for half in range(2):
                    if (direction, half) in ring_moves(step):
                        ring_copy(l, direction, step, half).wait_send()


def collect(learner_flat, param_offsets, owner_map, slice_map):
    x = learner_flat.reshape(LAYERS, SHARD_ROWS, LANES).transpose(1, 0, 2).reshape(LAYERS * SHARD_ROWS, LANES)
    vmem = pl.BlockSpec(memory_space=pltpu.VMEM)
    dma = pltpu.SemaphoreType.DMA
    ring = (LAYERS, 2, STEPS, 2)
    chunk = pltpu.VMEM((FSDP, 4, 8, LANES), BF16)
    rows = pltpu.VMEM((TP, 4 * QUARTER, 8, LANES), BF16)
    rest = pltpu.VMEM((TP, QUARTER, 2, 8, LANES), BF16)
    return pl.pallas_call(
        refresh_kernel,
        out_shape=(
            jax.ShapeDtypeStruct((LAYERS, PER_GROUP, ROWS_Q, LANES), BF16),
            jax.ShapeDtypeStruct((LAYERS, PER_GROUP, ROWS_O, LANES), BF16),
            jax.ShapeDtypeStruct((LAYERS, PER_GROUP, QK_NOPE, KVR), BF16),
            jax.ShapeDtypeStruct((LAYERS, PER_GROUP, V_DIM, KVR), BF16),
        ),
        in_specs=[pl.BlockSpec(memory_space=pltpu.HBM)] * 4,
        out_specs=(vmem,) * 4,
        scratch_shapes=[chunk] * (2 * CHUNKS)
        + [rows] * (2 * CHUNKS)
        + [pltpu.VMEM((FSDP, 2, 8, LANES), BF16)] * LAYERS
        + [pltpu.VMEM((TP, FSDP, 2, 8, LANES), BF16)] * LAYERS
        + [pltpu.VMEM((FSDP, TP, 2, 8, LANES), BF16)] * LAYERS
        + [
            pltpu.VMEM((FSDP, LAYERS, 8, LANES), BF16),
            pltpu.VMEM((FSDP, LAYERS, 8, LANES), BF16),
            rest,
            rest,
            pltpu.VMEM((LAYERS * SHARD_ROWS, LANES), BF16),
            pltpu.VMEM((LAYERS * SHARD_ROWS + 2 * PAD, LANES), F32),
            pltpu.VMEM((LAYERS * 4, HEADS), jnp.int32),
            pltpu.SMEM((LAYERS * 4, HEADS), jnp.int32),
            pltpu.VMEM((ROWS_O, LANES), F32),
            pltpu.VMEM((ROWS_Q, LANES), F32),
            pltpu.VMEM((TP * FSDP * 16 + 16 * TP, LANES), F32),
            pltpu.VMEM((QK_NOPE + 8, LANES), F32),
            pltpu.SMEM((TP, FSDP), jnp.int32),
            pltpu.VMEM((LAYERS, HEADS), jnp.int32),
            pltpu.VMEM((LAYERS, 4, HEADS), jnp.int32),
            dma((LOADS,)), dma, dma((CHUNKS,)), dma((CHUNKS,)), dma((CHUNKS,)), dma((CHUNKS,)), dma((1,)), dma((1,)),
            dma((1,)), dma((1,)), dma((LAYERS,)), dma((LAYERS,)), dma(ring), dma(ring), dma((LAYERS,)),
            pltpu.SemaphoreType.REGULAR((STEPS - 1,)), dma((3,)),
        ],
        compiler_params=pltpu.CompilerParams(collective_id=0, has_side_effects=True, vmem_limit_bytes=32 << 20),
    )(*(pltpu.with_memory_space_constraint(a, pltpu.HBM) for a in (slice_map.T, owner_map, param_offsets.transpose(0, 2, 1), x)))


def product_kernel(q_ref, o_ref, k_ref, v_ref, q_out, o_out, q_buf, o_buf, q_sem, o_sem):
    def leave(i):
        l, j, at = i // PER_GROUP, i % PER_GROUP, i
        return (
            pltpu.make_async_copy(o_buf.at[at], o_out.at[l, j], o_sem.at[at]),
            pltpu.make_async_copy(q_buf.at[at], q_out.at[l, j], q_sem.at[at]),
        )

    for i in range(CHUNKS):
        l, j, at = i // PER_GROUP, i % PER_GROUP, i
        q_buf[at] = jnp.dot(q_ref[l, j], k_ref[l, j], preferred_element_type=F32).astype(BF16)
        pltpu.make_async_copy(q_buf.at[at], q_out.at[l, j], q_sem.at[at]).start()
        for r in range(0, ROWS_O, 224):
            o_buf[at, pl.ds(r, 224)] = jnp.dot(o_ref[l, j, pl.ds(r, 224)], v_ref[l, j], preferred_element_type=F32).astype(BF16)
            pltpu.make_async_copy(o_buf.at[at, pl.ds(r, 224)], o_out.at[l, j, pl.ds(r, 224)], o_sem.at[at]).start()
    for i in range(CHUNKS):
        for copy in leave(i):
            copy.wait()


def products(query, out, key, value):
    vmem = pl.BlockSpec(memory_space=pltpu.VMEM)
    hbm = pl.BlockSpec(memory_space=pltpu.HBM)
    return pl.pallas_call(
        product_kernel,
        out_shape=(
            jax.ShapeDtypeStruct((LAYERS, PER_GROUP, ROWS_Q, KVR), BF16),
            jax.ShapeDtypeStruct((LAYERS, PER_GROUP, ROWS_O, KVR), BF16),
        ),
        in_specs=[vmem] * 4,
        out_specs=(hbm, hbm),
        scratch_shapes=[
            pltpu.VMEM((CHUNKS, ROWS_Q, KVR), BF16),
            pltpu.VMEM((CHUNKS, ROWS_O, KVR), BF16),
            pltpu.SemaphoreType.DMA((CHUNKS,)),
            pltpu.SemaphoreType.DMA((CHUNKS,)),
        ],
        compiler_params=pltpu.CompilerParams(vmem_limit_bytes=12 << 20),
    )(query, out, key, value)


def per_device(learner_flat, param_offsets, owner_map, slice_map):
    return products(*collect(learner_flat, param_offsets, owner_map, slice_map))


def solution(mesh):
    placed = (P(None, ("fsdp", "tp")), P(), P(), P())
    return jax.shard_map(
        per_device,
        mesh=mesh,
        in_specs=placed,
        out_specs=(P(None, "fsdp", "tp", None), P(None, "fsdp", "tp", None)),
        check_vma=False,
    )
```
